256 devices in a mesh: gx: 16 (over y, x), gy: 4 (over z_hi, core), gz: 4 (over z_lo).
Axes of the slice: x: 4, y: 4, z: 8 (z_hi: 2, z_lo: 4; z = z_hi * 4 + z_lo), core: 2. Of those that a mesh axis runs over, the one named last changes fastest.
Arguments:
- coarse_density: float32 [64, 32, 256], P('gx', 'gy', 'gz'), may hold values from 0.02 to 2
- atom_count: int32 [16, 16], P('gx', ('gy', 'gz')), may hold values from 1 to 16, 128 in all within a row
- atom_species: int32 [16, 16, 16], P('gx', ('gy', 'gz')), may hold values from 0 to 1
- density_matrix: float32 [16, 16, 16, 324], P('gx', ('gy', 'gz')), as said below
- partial_waves: float32 [2, 18, 5000], replicated, may hold values from -1.8 to 1.8
- smooth_waves: float32 [2, 18, 5000], replicated, may hold values from -1.8 to 1.8
- core_density: float32 [2, 100], replicated, may hold values from 0.05 to 2
- smooth_core: float32 [2, 100], replicated, may hold values from 0.05 to 2
Outputs:
- potential: float32 [128, 64, 512], P('gx', 'gy', 'gz')
- energy_density: float32 [128, 64, 512], P('gx', 'gy', 'gz')
- atom_hamiltonian: float32 [16, 16, 16, 324], P('gx', ('gy', 'gz'))
- atom_energy: float32 [16, 16, 16], P('gx', ('gy', 'gz'))
The draws below stay inside these ranges and needn't reach their ends.
Inputs may be any that keep to these rules, and one draw needn't show every extreme that they name: `atom_count`: the counts of the 16 domains that share one index of gx sum to 128, and in every such row the largest count is exactly 16. `density_matrix`: each slot holds a symmetric positive semidefinite 18 x 18 matrix.
All inputs are finite; a program needn't handle non-finite values.
Results may differ from the reference program's by a relative error of at most 0.0003.
Values sent between devices are 32-bit elements; how exact they have to be, the bound alone decides.
No kernel may reach another device: no remote copies, remote signals or barrier semaphores. Data moves between devices by JAX's collectives and lax.ppermute only.
A program may use at most 64 MiB of HBM per device.

```python
import math
import jax
import jax.numpy as jnp
import numpy as np
from jax import lax

MEAN = 8
NI = 18
NRAD = 100
NSPEC = 2
GROUP = 16
SLOTS = 16
NPTS = 5000
NX = 64
NY = 32
NZ = 256
N_GX = 16


def draw_density_matrix(key, part):
    out_shape = (N_GX, GROUP, SLOTS, NI, NI)
    factor = jax.random.normal(key, out_shape, jnp.float32)
    matrix = jnp.einsum('abcij,abckj->abcik', factor, factor) / NI
    return matrix.reshape(N_GX, GROUP, SLOTS, NI * NI)


def plant(array, own_key, smallest, high):
    dims = array.shape
    place = [jax.random.randint(jax.random.fold_in(own_key, axis), (), 0, dims[axis]) for axis in range(len(dims))]
    array = array.at[tuple(place)].set(smallest)
    longest = dims.index(max(dims))
    place[longest] = (place[longest] + 1) % dims[longest]
    return array.at[tuple(place)].set(high)


def levels(stream_key, extent, cuts, least, largest):
    gain, own = 1.0, jax.random.fold_in(stream_key, 6)
    for dim, shards_of in cuts:
        draws = jnp.exp(jax.random.uniform(jax.random.fold_in(own, dim), (shards_of,), jnp.float32, least / len(cuts), largest / len(cuts)))
        gain = gain * jnp.repeat(draws, extent[dim] // shards_of).reshape([-1 if axis == dim else 1 for axis in range(len(extent))])
    return gain


def split_up(number_of, total, bound, slope):
    weights = [(1 << 20) // math.isqrt(standing ** slope) + 1 for standing in range(2, number_of + 1)]
    surplus, counts = total - bound - (number_of - 1), [1] * (number_of - 1)
    while surplus > 0:
        movable = [i for i in range(number_of - 1) if counts[i] < bound]
        pool, remaining = sum([weights[i] for i in movable]), surplus
        for i in movable:
            addition = min(bound - counts[i], max(1, remaining * weights[i] // pool), surplus)
            counts[i] = counts[i] + addition
            surplus = surplus - addition
    return np.array([bound] + counts)


def ragged_sizes(own_key, count, total, bound, skew):
    if count == 2:
        one = jax.random.randint(own_key, (), max(1, total - bound), min(bound, total - 1) + 1)
        return jnp.stack([one, total - one])
    lengths = jnp.asarray(split_up(count, total, bound, skew), jnp.int32)
    twos = (count - 1) // 2
    source_of, sink = lengths[1:1 + 2 * twos:2], lengths[2:2 + 2 * twos:2]
    room = jnp.minimum(source_of - 1, bound - sink)
    shifted = jax.random.randint(jax.random.fold_in(own_key, 1), (twos,), 0, 1 << 20) % (room + 1)
    lengths = lengths.at[1:1 + 2 * twos:2].set(source_of - shifted).at[2:2 + 2 * twos:2].set(sink + shifted)
    return lengths[jax.random.permutation(jax.random.fold_in(own_key, 2), count)]


def scatter_about(key, extent, spread, bound, kind=jnp.bfloat16):
    return jnp.clip(spread * jax.random.normal(key, extent, jnp.float32), -bound, bound).astype(kind)


def setup_inputs(seed: int = 0) -> dict:
    key_of = jax.random.split(jax.random.key(seed), 9)
    return {
        "coarse_density": jnp.clip(jnp.exp(math.log(2.0) - 4.6051702 * jax.random.uniform(key_of[0], (NX, NY, NZ), jnp.float32) ** levels(key_of[0], (NX, NY, NZ), ((0, 16), (1, 4), (2, 4)), -0.2, 0.2)), 0.02, 2.0),
        "atom_count": jax.vmap(lambda own: ragged_sizes(own, GROUP, MEAN * GROUP, SLOTS, 2))(jax.random.split(key_of[1], N_GX)).reshape((N_GX, GROUP)).astype(jnp.int32),
        "atom_species": plant(jax.random.randint(key_of[2], (N_GX, GROUP, SLOTS), 0, 2), jax.random.fold_in(key_of[2], 1), 0, 1).astype(jnp.int32),
        "density_matrix": draw_density_matrix(jax.random.fold_in(key_of[8], 71), 0),
        "partial_waves": scatter_about(key_of[4], (NSPEC, NI, NPTS), 0.3, 1.8, jnp.float32),
        "smooth_waves": scatter_about(key_of[5], (NSPEC, NI, NPTS), 0.3, 1.8, jnp.float32),
        "core_density": jnp.clip(jnp.exp(jax.random.uniform(key_of[6], (NSPEC, NRAD), jnp.float32, math.log(0.05), math.log(2.0))), 0.05, 2.0),
        "smooth_core": jnp.clip(jnp.exp(jax.random.uniform(key_of[7], (NSPEC, NRAD), jnp.float32, math.log(0.05), math.log(2.0))), 0.05, 2.0),
    }


fine_step = 0.1
sphere_radius = 2.5
enhance_kappa = 0.804
enhance_mu = 0.2195149727645171
gradient_beta = 0.06672455060314922
gradient_gamma = (1.0 - math.log(2.0)) / math.pi ** 2
perdew_amplitude = 0.031091
perdew_alpha = 0.2137
perdew_first = 7.5957
perdew_second = 3.5876
perdew_third = 1.6382
perdew_fourth = 0.49294

def functional_energy(density, sigma_field):
    cube_root = jnp.cbrt(density)
    fermi_wave = (3.0 * math.pi ** 2) ** (1.0 / 3.0) * cube_root
    exchange = -0.75 * (3.0 / math.pi) ** (1.0 / 3.0) * cube_root
    squared_density = density * density
    reduced = sigma_field / (4.0 * fermi_wave * fermi_wave * squared_density)
    enhance = 1.0 + enhance_kappa - enhance_kappa / (1.0 + enhance_mu * reduced / enhance_kappa)
    radius = (3.0 / (4.0 * math.pi)) ** (1.0 / 3.0) / cube_root
    root_radius = jnp.sqrt(radius)
    fitted = 2.0 * perdew_amplitude * (perdew_first * root_radius + perdew_second * radius + perdew_third * radius * root_radius + perdew_fourth * radius * radius)
    correlation = -2.0 * perdew_amplitude * (1.0 + perdew_alpha * radius) * jnp.log1p(1.0 / fitted)
    screening = 4.0 * fermi_wave / math.pi
    scaled = sigma_field / (4.0 * screening * squared_density)
    factor = gradient_beta / gradient_gamma / jnp.expm1(-correlation / gradient_gamma)
    product = factor * scaled
    gradient_term = gradient_gamma * jnp.log1p(gradient_beta / gradient_gamma * scaled * (1.0 + product) / (1.0 + product + product * product))
    return density * (exchange * enhance + correlation + gradient_term)

def upsample_axis(values, direction):
    length = values.shape[direction]
    before_cell = lax.slice_in_dim(values, 0, length - 2, axis=direction)
    centre_cell = lax.slice_in_dim(values, 1, length - 1, axis=direction)
    after_cell = lax.slice_in_dim(values, 2, length, axis=direction)
    even_cells = 0.75 * centre_cell + 0.25 * before_cell
    odd_cells = 0.75 * centre_cell + 0.25 * after_cell
    paired = jnp.stack([even_cells, odd_cells], axis=direction + 1)
    new_shape = list(values.shape)
    new_shape[direction] = 2 * (length - 2)
    return paired.reshape(new_shape)

def upsample(values):
    for direction in range(3):
        values = upsample_axis(values, direction)
    return values

def radial_slope(values):
    first_diff = values[..., 1:2] - values[..., 0:1]
    middle_part = 0.5 * (values[..., 2:] - values[..., :-2])
    last_diff = values[..., -1:] - values[..., -2:-1]
    return jnp.concatenate([first_diff, middle_part, last_diff], axis=-1) * (values.shape[-1] / sphere_radius)

def atom_batch(matrices, species_ids, partial_waves, smooth_waves, core_density, smooth_core):
    batch_size = matrices.shape[0]
    width = partial_waves.shape[1]
    radial_points = core_density.shape[1]
    angular_points = partial_waves.shape[2] // radial_points
    radii_grid = sphere_radius * (jnp.arange(radial_points, dtype=jnp.float32) + 0.5) / radial_points
    weights = radii_grid * radii_grid * (sphere_radius / radial_points)
    is_first = species_ids == 0
    waves = jnp.where(is_first[:, None, None], partial_waves[0][None], partial_waves[1][None])
    smooth = jnp.where(is_first[:, None, None], smooth_waves[0][None], smooth_waves[1][None])
    core_values = jnp.where(is_first[:, None], core_density[0][None], core_density[1][None])
    smooth_values = jnp.where(is_first[:, None], smooth_core[0][None], smooth_core[1][None])

    def sphere_energy(flat_matrix, tables, cores_here):
        matrix = flat_matrix.reshape(batch_size, width, width)
        contracted = jnp.einsum('bij,bjq->biq', matrix, tables, precision=lax.Precision.HIGHEST)
        density = lax.optimization_barrier(jnp.sum(tables * contracted, axis=1)).reshape(batch_size, angular_points, radial_points) + cores_here[:, None, :]
        slope_values = radial_slope(density)
        return lax.optimization_barrier(jnp.sum(functional_energy(density, slope_values * slope_values) * weights, axis=(1, 2)))

    def correction(flat_matrix):
        return (sphere_energy(flat_matrix, waves, core_values) - sphere_energy(flat_matrix, smooth, smooth_values)) * (4.0 * math.pi / angular_points)
    energies, pullback = jax.vjp(correction, matrices)
    hamiltonian, = pullback(jnp.ones_like(energies))
    return (energies, hamiltonian)

def atom_terms(matrices, species_ids, partial_waves, smooth_waves, core_density, smooth_core):
    total_atoms = matrices.shape[0]
    pair_total = matrices.shape[1]
    group_size = math.gcd(total_atoms, 8)
    grouped = (matrices.reshape(total_atoms // group_size, group_size, pair_total), species_ids.reshape(total_atoms // group_size, group_size))

    def run_group(element):
        return atom_batch(element[0], element[1], partial_waves, smooth_waves, core_density, smooth_core)
    energies, hamiltonian = lax.map(run_group, grouped)
    return (energies.reshape(total_atoms), hamiltonian.reshape(total_atoms, pair_total))

def reference(coarse_density, atom_count, atom_species, density_matrix, partial_waves, smooth_waves, core_density, smooth_core):
    padded = jnp.pad(coarse_density, 1, mode='wrap')
    refined = upsample(padded)
    scale_back = 2.0 * fine_step
    gradient = [(jnp.roll(refined, -1, direction) - jnp.roll(refined, 1, direction)) / scale_back for direction in range(3)]
    sigma_field = gradient[0] * gradient[0] + gradient[1] * gradient[1] + gradient[2] * gradient[2]
    energy_density, pullback = jax.vjp(functional_energy, refined, sigma_field)
    by_density, by_sigma = pullback(jnp.ones_like(energy_density))
    flux_terms = [2.0 * by_sigma * gradient[direction] for direction in range(3)]
    spread_terms = [jnp.roll(flux_terms[direction], -1, direction) - jnp.roll(flux_terms[direction], 1, direction) for direction in range(3)]
    divergence = (spread_terms[0] + spread_terms[1] + spread_terms[2]) / scale_back
    potential = by_density - divergence
    slab_total = atom_count.shape[0]
    group_width = atom_count.shape[1]
    slot_total = density_matrix.shape[2]
    pair_total = density_matrix.shape[3]
    before = jnp.cumsum(atom_count, axis=1).astype(jnp.int32) - atom_count
    slot_ids = jnp.arange(slot_total, dtype=jnp.int32)
    occupied = slot_ids[None, None, :] < atom_count[:, :, None]
    position = before[:, :, None] + slot_ids[None, None, :]
    packed_total = slab_total * group_width * MEAN
    slab_ids = jnp.arange(slab_total, dtype=jnp.int32)[:, None, None]
    destination = jnp.where(occupied, slab_ids * (group_width * MEAN) + position, packed_total).reshape(-1).astype(jnp.int32)
    packed = jnp.zeros((packed_total, pair_total), jnp.float32).at[destination].set(density_matrix.reshape(-1, pair_total), mode='drop')
    packed_species = jnp.zeros((packed_total,), jnp.int32).at[destination].set(atom_species.reshape(-1), mode='drop')
    energies, hamiltonian = atom_terms(packed, packed_species, partial_waves, smooth_waves, core_density, smooth_core)
    lookup = jnp.minimum(destination, packed_total - 1).astype(jnp.int32)
    flat_occupied = occupied.reshape(-1)
    atom_hamiltonian = jnp.where(flat_occupied[:, None], hamiltonian[lookup], 0.0).reshape(density_matrix.shape)
    atom_energy = jnp.where(flat_occupied, energies[lookup], 0.0).reshape(atom_species.shape)
    return (potential, energy_density, atom_hamiltonian, atom_energy)
```

```python
import math

import jax
import jax.numpy as jnp
from jax import lax
from jax.sharding import PartitionSpec as P

fine_step = 0.1
sphere_radius = 2.5
enhance_kappa = 0.804
enhance_mu = 0.2195149727645171
gradient_beta = 0.06672455060314922
gradient_gamma = (1.0 - math.log(2.0)) / math.pi**2
perdew_amplitude = 0.031091
perdew_alpha = 0.2137
perdew_first = 7.5957
perdew_second = 3.5876
perdew_third = 1.6382
perdew_fourth = 0.49294


def with_halo(cells, sides, width):
    for axis, dim in sides:
        count = lax.axis_size(axis)
        even = lax.axis_index(axis) % 2 == 0
        head = lax.slice_in_dim(cells, 0, width, axis=dim)
        tail = lax.slice_in_dim(cells, cells.shape[dim] - width, cells.shape[dim], axis=dim)
        inner = [(i, i ^ 1) for i in range(count)]
        outer = [(i, (i + 1 if i % 2 else i - 1) % count) for i in range(count)]
        first = lax.ppermute(jnp.where(even, tail, head), axis, inner)
        second = lax.ppermute(jnp.where(even, head, tail), axis, outer)
        cells = jnp.concatenate(
            [jnp.where(even, second, first), cells, jnp.where(even, first, second)], axis=dim
        )
    return cells


def functional_energy(density, sigma_field):
    cube_root = jnp.cbrt(density)
    fermi_wave = (3.0 * math.pi**2) ** (1.0 / 3.0) * cube_root
    exchange = -0.75 * (3.0 / math.pi) ** (1.0 / 3.0) * cube_root
    squared_density = density * density
    reduced = sigma_field / (4.0 * fermi_wave * fermi_wave * squared_density)
    enhance = 1.0 + enhance_kappa - enhance_kappa / (1.0 + enhance_mu * reduced / enhance_kappa)
    radius = (3.0 / (4.0 * math.pi)) ** (1.0 / 3.0) / cube_root
    root_radius = jnp.sqrt(radius)
    fitted = (
        2.0
        * perdew_amplitude
        * (
            perdew_first * root_radius
            + perdew_second * radius
            + perdew_third * radius * root_radius
            + perdew_fourth * radius * radius
        )
    )
    correlation = -2.0 * perdew_amplitude * (1.0 + perdew_alpha * radius) * jnp.log1p(1.0 / fitted)
    screening = 4.0 * fermi_wave / math.pi
    scaled = sigma_field / (4.0 * screening * squared_density)
    factor = gradient_beta / gradient_gamma / jnp.expm1(-correlation / gradient_gamma)
    product = factor * scaled
    gradient_term = gradient_gamma * jnp.log1p(
        gradient_beta
        / gradient_gamma
        * scaled
        * (1.0 + product)
        / (1.0 + product + product * product)
    )
    return density * (exchange * enhance + correlation + gradient_term)


def upsample_axis(values, direction):
    length = values.shape[direction]
    before_cell = lax.slice_in_dim(values, 0, length - 2, axis=direction)
    centre_cell = lax.slice_in_dim(values, 1, length - 1, axis=direction)
    after_cell = lax.slice_in_dim(values, 2, length, axis=direction)
    even_cells = 0.75 * centre_cell + 0.25 * before_cell
    odd_cells = 0.75 * centre_cell + 0.25 * after_cell
    paired = jnp.stack([even_cells, odd_cells], axis=direction + 1)
    new_shape = list(values.shape)
    new_shape[direction] = 2 * (length - 2)
    return paired.reshape(new_shape)


def upsample(values):
    for direction in range(3):
        values = upsample_axis(values, direction)
    return values


def grid_fields(extended):
    scale_back = 2.0 * fine_step
    interior = extended[1:-1, 1:-1, 1:-1]
    gradient = [
        (extended[2:, 1:-1, 1:-1] - extended[:-2, 1:-1, 1:-1]) / scale_back,
        (extended[1:-1, 2:, 1:-1] - extended[1:-1, :-2, 1:-1]) / scale_back,
        (extended[1:-1, 1:-1, 2:] - extended[1:-1, 1:-1, :-2]) / scale_back,
    ]
    sigma_field = gradient[0] * gradient[0] + gradient[1] * gradient[1] + gradient[2] * gradient[2]
    energy_values, pullback = jax.vjp(functional_energy, interior, sigma_field)
    by_density, by_sigma = pullback(jnp.ones_like(energy_values))
    flux_terms = [2.0 * by_sigma * gradient[direction] for direction in range(3)]
    divergence = (
        flux_terms[0][2:, 1:-1, 1:-1]
        - flux_terms[0][:-2, 1:-1, 1:-1]
        + (flux_terms[1][1:-1, 2:, 1:-1] - flux_terms[1][1:-1, :-2, 1:-1])
        + (flux_terms[2][1:-1, 1:-1, 2:] - flux_terms[2][1:-1, 1:-1, :-2])
    ) / scale_back
    return (by_density[1:-1, 1:-1, 1:-1] - divergence, energy_values[1:-1, 1:-1, 1:-1])


def radial_slope(values):
    first_diff = values[..., 1:2] - values[..., 0:1]
    middle_part = 0.5 * (values[..., 2:] - values[..., :-2])
    last_diff = values[..., -1:] - values[..., -2:-1]
    return jnp.concatenate([first_diff, middle_part, last_diff], axis=-1) * (
        values.shape[-1] / sphere_radius
    )


def atom_batch(matrices, species_ids, partial_waves, smooth_waves, core_density, smooth_core):
    batch_size = matrices.shape[0]
    width = partial_waves.shape[1]
    radial_points = core_density.shape[1]
    angular_points = partial_waves.shape[2] // radial_points
    radii_grid = (
        sphere_radius * (jnp.arange(radial_points, dtype=jnp.float32) + 0.5) / radial_points
    )
    weights = radii_grid * radii_grid * (sphere_radius / radial_points)
    is_first = species_ids == 0
    waves = jnp.where(is_first[:, None, None], partial_waves[0][None], partial_waves[1][None])
    smooth = jnp.where(is_first[:, None, None], smooth_waves[0][None], smooth_waves[1][None])
    core_values = jnp.where(is_first[:, None], core_density[0][None], core_density[1][None])
    smooth_values = jnp.where(is_first[:, None], smooth_core[0][None], smooth_core[1][None])

    def sphere_energy(flat_matrix, tables, cores_here):
        matrix = flat_matrix.reshape(batch_size, width, width)
        contracted = jnp.einsum("bij,bjq->biq", matrix, tables, precision=lax.Precision.HIGHEST)
        density = (
            jnp.sum(tables * contracted, axis=1).reshape(batch_size, angular_points, radial_points)
            + cores_here[:, None, :]
        )
        slope_values = radial_slope(density)
        return jnp.sum(
            functional_energy(density, slope_values * slope_values) * weights, axis=(1, 2)
        )

    def correction(flat_matrix):
        return (
            sphere_energy(flat_matrix, waves, core_values)
            - sphere_energy(flat_matrix, smooth, smooth_values)
        ) * (4.0 * math.pi / angular_points)

    energies, pullback = jax.vjp(correction, matrices)
    (hamiltonian,) = pullback(jnp.ones_like(energies))
    return (energies, hamiltonian)


def shards(
    coarse_density,
    atom_count,
    atom_species,
    density_matrix,
    partial_waves,
    smooth_waves,
    core_density,
    smooth_core,
):
    rimmed = with_halo(coarse_density, (("gy", 1), ("gx", 0), ("gz", 2)), 2)
    fine = upsample(rimmed)
    potential, energy_density = grid_fields(fine)
    slot_total = density_matrix.shape[2]
    pair_total = density_matrix.shape[3]
    matrices = density_matrix.reshape(slot_total, pair_total)
    species_ids = atom_species.reshape(slot_total)
    occupied = jnp.arange(slot_total, dtype=jnp.int32) < atom_count.reshape(())
    energies, hamiltonian = atom_batch(
        matrices, species_ids, partial_waves, smooth_waves, core_density, smooth_core
    )
    placed = jnp.where(occupied[:, None], hamiltonian, 0.0)
    placed_energy = jnp.where(occupied, energies, 0.0)
    return (
        potential,
        energy_density,
        placed.reshape(density_matrix.shape),
        placed_energy.reshape(atom_species.shape),
    )


def solution(mesh):
    in_specs = (
        P("gx", "gy", "gz"),
        P("gx", ("gy", "gz")),
        P("gx", ("gy", "gz"), None),
        P("gx", ("gy", "gz"), None, None),
        P(),
        P(),
        P(),
        P(),
    )
    out_specs = (
        P("gx", "gy", "gz"),
        P("gx", "gy", "gz"),
        P("gx", ("gy", "gz"), None, None),
        P("gx", ("gy", "gz"), None),
    )
    return jax.shard_map(shards, mesh=mesh, in_specs=in_specs, out_specs=out_specs, check_vma=False)
```

```python
import functools
import math

import jax
import jax.numpy as jnp
import numpy as np
from jax import lax
from jax.experimental import pallas as pl
from jax.experimental.pallas import tpu as pltpu
from jax.sharding import PartitionSpec as P

fine_step = 0.1
sphere_radius = 2.5
enhance_kappa = 0.804
enhance_mu = 0.2195149727645171
gradient_beta = 0.06672455060314922
gradient_gamma = (1.0 - math.log(2.0)) / math.pi**2
perdew_amplitude = 0.031091
perdew_alpha = 0.2137
perdew_first = 7.5957
perdew_second = 3.5876
perdew_third = 1.6382
perdew_fourth = 0.49294

exchange_scale = -0.75 * (3.0 / math.pi) ** (1.0 / 3.0)
fermi_scale = (3.0 * math.pi**2) ** (1.0 / 3.0)
radius_scale = (3.0 / (4.0 * math.pi)) ** (1.0 / 3.0)
reduced_scale = 1.0 / (4.0 * fermi_scale**2)
scaled_scale = math.pi / (16.0 * fermi_scale)
beta_ratio = gradient_beta / gradient_gamma
fit = [
    2.0 * perdew_amplitude * c * radius_scale ** (k / 2.0)
    for k, c in ((1, perdew_first), (2, perdew_second), (3, perdew_third), (4, perdew_fourth))
]
ln2 = math.log(2.0)


def functional(n, s):
    m = jnp.exp2(jnp.log2(n) * (-1.0 / 6.0))
    m2 = m * m
    m4 = m2 * m2
    m8 = m4 * m4
    m14 = m8 * m4 * m2
    m16 = m8 * m8
    fitted = m * (fit[0] + m * (fit[1] + m * (fit[2] + m * fit[3])))
    slope = m * (fit[0] + m * (2.0 * fit[1] + m * (3.0 * fit[2] + m * (4.0 * fit[3]))))
    one_fit = 1.0 + fitted
    enhance = 1.0 + (enhance_mu / enhance_kappa * reduced_scale) * (s * m16)
    fit_both = fitted * one_fit
    joint = 1.0 / (fit_both * enhance)
    inverse_fit = joint * enhance
    damp = joint * fit_both
    log_term = jnp.log2(1.0 + one_fit * inverse_fit)
    alpha_r = (perdew_alpha * radius_scale) * m2
    one_alpha = 1.0 + alpha_r
    product_c = one_alpha * log_term
    c = (-2.0 * perdew_amplitude * ln2) * product_c
    inv_exp = 1.0 / (jnp.exp2((2.0 * perdew_amplitude / gradient_gamma) * product_c) - 1.0)
    c_n = (2.0 * perdew_amplitude / 3.0) * (
        ln2 * alpha_r * log_term - 0.5 * one_alpha * slope * inverse_fit
    )
    b = beta_ratio * inv_exp
    t = scaled_scale * (s * m14)
    q = b * t
    num = 1.0 + q
    den_inv = 1.0 / (1.0 + q * num)
    z = 1.0 + (beta_ratio * t) * (num * den_inv)
    z_inv = 1.0 / z
    h = (gradient_gamma * ln2) * jnp.log2(z)
    den_z = den_inv * z_inv
    h_t = gradient_beta * ((num + q) * den_inv) * den_z
    h_c = (t * (q * den_inv)) * ((q * (1.0 + num)) * den_z) * (b + beta_ratio)
    x = exchange_scale * (n * m4)
    xf = x * ((1.0 + enhance_kappa) - enhance_kappa * damp)
    damp2 = damp * damp
    xfp = (enhance_kappa * x) * (damp - damp2)
    e = n * (xf + c + h)
    e_n = (4.0 / 3.0) * xf - (8.0 / 3.0) * xfp + (c + h) + (1.0 - h_c) * c_n - (7.0 / 3.0) * (h_t * t)
    e_s = n * ((enhance_mu * reduced_scale) * (x * damp2 * m16) + scaled_scale * (h_t * m14))
    return e, e_n, e_s


ROW = 24


def radial_table(nrad, npts, width):
    g = np.arange(width) % nrad
    live = np.arange(width) < npts
    r = sphere_radius * (g + 0.5) / nrad
    w = r * r * (sphere_radius / nrad)
    k = nrad / sphere_radius
    up = np.where(g == nrad - 1, 0.0, np.where(g == 0, k, 0.5 * k))
    down = np.where(g == 0, 0.0, np.where(g == nrad - 1, -k, -0.5 * k))
    mid = np.where(g == 0, -k, np.where(g == nrad - 1, k, 0.0))
    rows = np.stack([w, up, mid, down] + [np.zeros(width)] * 4) * live
    return rows.astype(np.float32)


def atoms_kernel(
    ni, nrad, npts, na, width, chunk, sub,
    count_ref, species_ref, d_ref, ae_ref, ps_ref, ae_core_ref, ps_core_ref, radial_ref,
    h_ref, e_ref,
    lhs32, waves, packed, cores, rho, part_n, part_q, grads, total,
):
    f32, bf16 = jnp.float32, jnp.bfloat16
    tiles = width // 128
    row = lax.broadcasted_iota(jnp.int32, (na, 128), 0)
    species = jnp.zeros((na, 128), jnp.int32)
    for a in range(na):
        species = jnp.where(row == a, species_ref[0, 0, a], species)
    first = species == 0
    first_f = jnp.where(first, 1.0, 0.0).astype(f32)
    second_f = 1.0 - first_f

    lhs32[...] = jnp.zeros_like(lhs32)
    for i in range(ni):
        d = d_ref[:, ni * i : ni * (i + 1)]
        d1 = d.astype(bf16).astype(f32)
        d2 = d - d1
        here = pl.ds(na * i, na)
        for block, part in ((0, d1), (1, d1), (2, d2)):
            at = 2 * ROW * block
            lhs32[here, at : at + ni] = part * first_f[:, :ni]
            lhs32[here, at + ROW : at + ROW + ni] = part * second_f[:, :ni]

    cores[...] = jnp.zeros_like(cores)
    cores[0:2, 0:nrad] = ae_core_ref[...]
    cores[2:4, 0:nrad] = ps_core_ref[...]
    line = cores[...]
    lane = lax.broadcasted_iota(jnp.int32, (8, width), 1)
    reach = nrad
    while reach < width:
        line = jnp.where(lane < reach, line, pltpu.roll(line, reach, 1))
        reach *= 2
    cores[...] = line

    waves[...] = jnp.zeros_like(waves)
    e_total = jnp.zeros((na, 128), f32)
    rho[...] = jnp.ones_like(rho)
    part_q[...] = jnp.zeros_like(part_q)

    for table, x_ref in enumerate((ae_ref, ps_ref)):
        sign = 1.0 if table == 0 else -1.0
        scale = sign * 4.0 * math.pi * nrad / npts
        waves[0:ni, 0:npts] = x_ref[0]
        waves[ROW : ROW + ni, 0:npts] = x_ref[1]

        def wide_first(cols):
            return jnp.concatenate([first] * (cols // 128), axis=1)

        def density(k, _):
            at = pl.multiple_of(k * chunk, chunk)
            x = waves[:, pl.ds(at, chunk)]
            x1 = x.astype(bf16)
            x2 = (x - x1.astype(f32)).astype(bf16)
            right = jnp.concatenate([x1, x2, x1], axis=0)
            packed[0 : 4 * ROW, pl.ds(at, chunk)] = right[0 : 4 * ROW]
            mixed = jnp.dot(
                lhs32[:, 0 : 6 * ROW].astype(bf16), right, preferred_element_type=f32
            )
            pick = wide_first(chunk)
            value = jnp.where(
                pick,
                cores[2 * table : 2 * table + 1, pl.ds(at, chunk)],
                cores[2 * table + 1 : 2 * table + 2, pl.ds(at, chunk)],
            )
            for i in range(ni):
                own = jnp.where(pick, x[i : i + 1], x[ROW + i : ROW + i + 1])
                value = value + own * mixed[na * i : na * (i + 1)]
            rho[:, pl.ds(pl.multiple_of(at + 128, 128), chunk)] = value
            return 0

        lax.fori_loop(0, width // chunk, density, 0)

        def local(k, e_sum):
            at = pl.multiple_of(k * sub, sub)
            wide = rho[:, pl.ds(at, sub + 256)]
            n = wide[:, 128 : 128 + sub]
            after = pltpu.roll(wide, sub + 255, 1)[:, 128 : 128 + sub]
            before = pltpu.roll(wide, 1, 1)[:, 128 : 128 + sub]
            here = pl.ds(at, sub)
            weight = radial_ref[0:1, here]
            up, mid, down = radial_ref[1:2, here], radial_ref[2:3, here], radial_ref[3:4, here]
            slope = up * after + mid * n + down * before
            e, e_n, e_s = functional(n, slope * slope)
            weight = weight * scale
            we = e * weight
            for j in range(sub // 128):
                e_sum = e_sum + we[:, 128 * j : 128 * (j + 1)]
            part_n[:, here] = e_n * weight
            part_q[:, pl.ds(pl.multiple_of(at + 128, 128), sub)] = 2.0 * slope * e_s * weight
            return e_sum

        e_total = lax.fori_loop(0, width // sub, local, e_total)

        def back(k, _):
            at = pl.multiple_of(k * chunk, chunk)
            here = pl.ds(at, chunk)
            around = pl.ds(pl.multiple_of(at, 128), chunk + 256)
            wide = part_q[:, around]
            n_part = part_n[:, here]
            after = pltpu.roll(wide, chunk + 255, 1)[:, 128 : 128 + chunk]
            before = pltpu.roll(wide, 1, 1)[:, 128 : 128 + chunk]
            g = (
                n_part
                + radial_ref[5:6, here] * before
                + radial_ref[2:3, here] * wide[:, 128 : 128 + chunk]
                + radial_ref[6:7, here] * after
            )
            pick = wide_first(chunk)
            x = waves[:, here]
            for i in range(ni):
                own = jnp.where(pick, x[i : i + 1], x[ROW + i : ROW + i + 1]) * g
                hi = own.astype(bf16)
                grads[na * i : na * (i + 1), :] = hi
                grads[na * (ni + i) : na * (ni + i + 1), :] = (own - hi.astype(f32)).astype(bf16)
            out = lax.dot_general(
                grads[...], packed[0 : 4 * ROW, here], (((1,), (1,)), ((), ())),
                preferred_element_type=f32,
            )
            if table == 0:
                @pl.when(k == 0)
                def _():
                    total[...] = out

                @pl.when(k != 0)
                def _():
                    total[...] += out
            else:
                total[...] += out
            return 0

        lax.fori_loop(0, width // chunk, back, 0)

    tally = count_ref[0, 0]
    live = row < tally
    for i in range(ni):
        hi = total[na * i : na * (i + 1), :]
        lo = total[na * (ni + i) : na * (ni + i + 1), :]
        both = hi + lo
        value = both[:, 0 : 2 * ROW] + both[:, 2 * ROW : 4 * ROW]
        value = jnp.where(first[:, :ni], value[:, 0:ni], value[:, ROW : ROW + ni])
        h_ref[:, ni * i : ni * (i + 1)] = jnp.where(live[:, :ni], value, 0.0)
    energy = jnp.sum(e_total, axis=1, keepdims=True)
    energy = jnp.where(live[:, :1], energy, 0.0)
    diagonal = lax.broadcasted_iota(jnp.int32, (na, na), 0) == lax.broadcasted_iota(
        jnp.int32, (na, na), 1
    )
    e_ref[...] = jnp.sum(jnp.where(diagonal, energy, 0.0), axis=0, keepdims=True)


def atom_terms(count, species, matrices, ae, ps, ae_core, ps_core, chunk=2560, sub=1280):
    na, pairs = matrices.shape
    ni, npts = ae.shape[1], ae.shape[2]
    nrad = ae_core.shape[1]
    width = -(-npts // chunk) * chunk
    radial = radial_table(nrad, npts, width)
    radial[5] = np.roll(radial[1], 1)
    radial[6] = np.roll(radial[3], -1)
    vmem = pl.BlockSpec(memory_space=pltpu.VMEM)
    smem = pl.BlockSpec(memory_space=pltpu.SMEM)
    f32, bf16 = jnp.float32, jnp.bfloat16
    return pl.pallas_call(
        functools.partial(atoms_kernel, ni, nrad, npts, na, width, chunk, sub),
        out_shape=(
            jax.ShapeDtypeStruct((na, pairs), f32),
            jax.ShapeDtypeStruct((1, na), f32),
        ),
        in_specs=[smem, smem] + [vmem] * 6,
        out_specs=(vmem, vmem),
        scratch_shapes=[
            pltpu.VMEM((na * ni, 256), f32),
            pltpu.VMEM((2 * ROW, width), f32),
            pltpu.VMEM((4 * ROW, width), bf16),
            pltpu.VMEM((8, width), f32),
            pltpu.VMEM((na, width + 256), f32),
            pltpu.VMEM((na, width), f32),
            pltpu.VMEM((na, width + 256), f32),
            pltpu.VMEM((2 * na * ni, chunk), bf16),
            pltpu.VMEM((2 * na * ni, 4 * ROW), f32),
        ],
        compiler_params=pltpu.CompilerParams(vmem_limit_bytes=48 << 20),
        cost_estimate=pl.CostEstimate(
            flops=4 * na * ni * ni * npts * 2, transcendentals=na * npts * 10, bytes_accessed=3 << 20
        ),
        name="atoms",
    )(count, species, matrices, ae, ps, ae_core, ps_core, jnp.asarray(radial))


def with_halo(cells, sides, width):
    for axis, dim in sides:
        count = lax.axis_size(axis)
        even = lax.axis_index(axis) % 2 == 0
        head = lax.slice_in_dim(cells, 0, width, axis=dim)
        tail = lax.slice_in_dim(cells, cells.shape[dim] - width, cells.shape[dim], axis=dim)
        inner = [(i, i ^ 1) for i in range(count)]
        outer = [(i, (i + 1 if i % 2 else i - 1) % count) for i in range(count)]
        first = lax.ppermute(jnp.where(even, tail, head), axis, inner)
        second = lax.ppermute(jnp.where(even, head, tail), axis, outer)
        cells = jnp.concatenate(
            [jnp.where(even, second, first), cells, jnp.where(even, first, second)], axis=dim
        )
    return cells


def upsample_axis(values, direction):
    length = values.shape[direction]
    before_cell = lax.slice_in_dim(values, 0, length - 2, axis=direction)
    centre_cell = lax.slice_in_dim(values, 1, length - 1, axis=direction)
    after_cell = lax.slice_in_dim(values, 2, length, axis=direction)
    even_cells = 0.75 * centre_cell + 0.25 * before_cell
    odd_cells = 0.75 * centre_cell + 0.25 * after_cell
    paired = jnp.stack([even_cells, odd_cells], axis=direction + 1)
    new_shape = list(values.shape)
    new_shape[direction] = 2 * (length - 2)
    return paired.reshape(new_shape)


def upsample(values):
    for direction in range(3):
        values = upsample_axis(values, direction)
    return values


def grid_fields(extended):
    scale_back = 2.0 * fine_step
    interior = extended[1:-1, 1:-1, 1:-1]
    gradient = [
        (extended[2:, 1:-1, 1:-1] - extended[:-2, 1:-1, 1:-1]) / scale_back,
        (extended[1:-1, 2:, 1:-1] - extended[1:-1, :-2, 1:-1]) / scale_back,
        (extended[1:-1, 1:-1, 2:] - extended[1:-1, 1:-1, :-2]) / scale_back,
    ]
    sigma_field = gradient[0] * gradient[0] + gradient[1] * gradient[1] + gradient[2] * gradient[2]
    energy_values, by_density, by_sigma = functional(interior, sigma_field)
    flux_terms = [2.0 * by_sigma * gradient[direction] for direction in range(3)]
    divergence = (
        flux_terms[0][2:, 1:-1, 1:-1]
        - flux_terms[0][:-2, 1:-1, 1:-1]
        + (flux_terms[1][1:-1, 2:, 1:-1] - flux_terms[1][1:-1, :-2, 1:-1])
        + (flux_terms[2][1:-1, 1:-1, 2:] - flux_terms[2][1:-1, 1:-1, :-2])
    ) / scale_back
    return (by_density[1:-1, 1:-1, 1:-1] - divergence, energy_values[1:-1, 1:-1, 1:-1])


def shards(
    coarse_density,
    atom_count,
    atom_species,
    density_matrix,
    partial_waves,
    smooth_waves,
    core_density,
    smooth_core,
):
    rimmed = with_halo(coarse_density, (("gy", 1), ("gx", 0), ("gz", 2)), 2)
    fine = upsample(rimmed)
    potential, energy_density = grid_fields(fine)
    slot_total, pair_total = density_matrix.shape[2:]
    placed, placed_energy = atom_terms(
        atom_count,
        atom_species,
        density_matrix.reshape(slot_total, pair_total),
        partial_waves,
        smooth_waves,
        core_density,
        smooth_core,
    )
    return (
        potential,
        energy_density,
        placed.reshape(density_matrix.shape),
        placed_energy.reshape(atom_species.shape),
    )


def solution(mesh):
    in_specs = (
        P("gx", "gy", "gz"),
        P("gx", ("gy", "gz")),
        P("gx", ("gy", "gz"), None),
        P("gx", ("gy", "gz"), None, None),
        P(),
        P(),
        P(),
        P(),
    )
    out_specs = (
        P("gx", "gy", "gz"),
        P("gx", "gy", "gz"),
        P("gx", ("gy", "gz"), None, None),
        P("gx", ("gy", "gz"), None),
    )
    return jax.shard_map(shards, mesh=mesh, in_specs=in_specs, out_specs=out_specs, check_vma=False)
```

```python
import functools
import math

import jax
import jax.numpy as jnp
import numpy as np
from jax import lax
from jax.experimental import pallas as pl
from jax.experimental.pallas import tpu as pltpu
from jax.sharding import PartitionSpec as P

fine_step = 0.1
sphere_radius = 2.5
enhance_kappa = 0.804
enhance_mu = 0.2195149727645171
gradient_beta = 0.06672455060314922
gradient_gamma = (1.0 - math.log(2.0)) / math.pi**2
perdew_amplitude = 0.031091
perdew_alpha = 0.2137
perdew_first = 7.5957
perdew_second = 3.5876
perdew_third = 1.6382
perdew_fourth = 0.49294

exchange_scale = -0.75 * (3.0 / math.pi) ** (1.0 / 3.0)
fermi_scale = (3.0 * math.pi**2) ** (1.0 / 3.0)
radius_scale = (3.0 / (4.0 * math.pi)) ** (1.0 / 3.0)
reduced_scale = 1.0 / (4.0 * fermi_scale**2)
scaled_scale = math.pi / (16.0 * fermi_scale)
beta_ratio = gradient_beta / gradient_gamma
fit = [
    2.0 * perdew_amplitude * c * radius_scale ** (k / 2.0)
    for k, c in ((1, perdew_first), (2, perdew_second), (3, perdew_third), (4, perdew_fourth))
]
ln2 = math.log(2.0)


def functional(n, s):
    m = jnp.exp2(jnp.log2(n) * (-1.0 / 6.0))
    m2 = m * m
    m4 = m2 * m2
    m8 = m4 * m4
    m14 = m8 * m4 * m2
    m16 = m8 * m8
    fitted = m * (fit[0] + m * (fit[1] + m * (fit[2] + m * fit[3])))
    slope = m * (fit[0] + m * (2.0 * fit[1] + m * (3.0 * fit[2] + m * (4.0 * fit[3]))))
    one_fit = 1.0 + fitted
    enhance = 1.0 + (enhance_mu / enhance_kappa * reduced_scale) * (s * m16)
    fit_both = fitted * one_fit
    joint = 1.0 / (fit_both * enhance)
    inverse_fit = joint * enhance
    damp = joint * fit_both
    log_term = jnp.log2(1.0 + one_fit * inverse_fit)
    alpha_r = (perdew_alpha * radius_scale) * m2
    one_alpha = 1.0 + alpha_r
    product_c = one_alpha * log_term
    c = (-2.0 * perdew_amplitude * ln2) * product_c
    inv_exp = 1.0 / (jnp.exp2((2.0 * perdew_amplitude / gradient_gamma) * product_c) - 1.0)
    c_n = (2.0 * perdew_amplitude / 3.0) * (
        ln2 * alpha_r * log_term - 0.5 * one_alpha * slope * inverse_fit
    )
    b = beta_ratio * inv_exp
    t = scaled_scale * (s * m14)
    q = b * t
    num = 1.0 + q
    den_inv = 1.0 / (1.0 + q * num)
    z = 1.0 + (beta_ratio * t) * (num * den_inv)
    z_inv = 1.0 / z
    h = (gradient_gamma * ln2) * jnp.log2(z)
    den_z = den_inv * z_inv
    h_t = gradient_beta * ((num + q) * den_inv) * den_z
    h_c = (t * (q * den_inv)) * ((q * (1.0 + num)) * den_z) * (b + beta_ratio)
    x = exchange_scale * (n * m4)
    xf = x * ((1.0 + enhance_kappa) - enhance_kappa * damp)
    damp2 = damp * damp
    xfp = (enhance_kappa * x) * (damp - damp2)
    e = n * (xf + c + h)
    e_n = (4.0 / 3.0) * xf - (8.0 / 3.0) * xfp + (c + h) + (1.0 - h_c) * c_n - (7.0 / 3.0) * (h_t * t)
    e_s = n * ((enhance_mu * reduced_scale) * (x * damp2 * m16) + scaled_scale * (h_t * m14))
    return e, e_n, e_s


ROW = 24


def radial_table(nrad, npts, width):
    g = np.arange(width) % nrad
    live = np.arange(width) < npts
    r = sphere_radius * (g + 0.5) / nrad
    w = r * r * (sphere_radius / nrad)
    k = nrad / sphere_radius
    up = np.where(g == nrad - 1, 0.0, np.where(g == 0, k, 0.5 * k))
    down = np.where(g == 0, 0.0, np.where(g == nrad - 1, -k, -0.5 * k))
    mid = np.where(g == 0, -k, np.where(g == nrad - 1, k, 0.0))
    rows = np.stack([w, up, mid, down] + [np.zeros(width)] * 4) * live
    return rows.astype(np.float32)


def atoms_kernel(
    ni, nrad, npts, na, width, chunk, sub,
    count_ref, species_ref, d_ref, ae_ref, ps_ref, ae_core_ref, ps_core_ref, radial_ref,
    h_ref, e_ref,
    lhs32, waves, packed, cores, rho, part_n, part_q, grads, total,
):
    f32, bf16 = jnp.float32, jnp.bfloat16
    tiles = width // 128
    row = lax.broadcasted_iota(jnp.int32, (na, 128), 0)
    species = jnp.zeros((na, 128), jnp.int32)
    for a in range(na):
        species = jnp.where(row == a, species_ref[0, 0, a], species)
    first = species == 0
    first_f = jnp.where(first, 1.0, 0.0).astype(f32)
    second_f = 1.0 - first_f

    lhs32[...] = jnp.zeros_like(lhs32)
    for i in range(ni):
        d = d_ref[:, ni * i : ni * (i + 1)]
        d1 = d.astype(bf16).astype(f32)
        d2 = d - d1
        here = pl.ds(na * i, na)
        for block, part in ((0, d1), (1, d1), (2, d2)):
            at = 2 * ROW * block
            lhs32[here, at : at + ni] = part * first_f[:, :ni]
            lhs32[here, at + ROW : at + ROW + ni] = part * second_f[:, :ni]

    cores[...] = jnp.zeros_like(cores)
    cores[0:2, 0:nrad] = ae_core_ref[...]
    cores[2:4, 0:nrad] = ps_core_ref[...]
    line = cores[...]
    lane = lax.broadcasted_iota(jnp.int32, (8, width), 1)
    reach = nrad
    while reach < width:
        line = jnp.where(lane < reach, line, pltpu.roll(line, reach, 1))
        reach *= 2
    cores[...] = line

    waves[...] = jnp.zeros_like(waves)
    e_total = jnp.zeros((na, 128), f32)
    rho[...] = jnp.ones_like(rho)
    part_q[...] = jnp.zeros_like(part_q)

    for table, x_ref in enumerate((ae_ref, ps_ref)):
        sign = 1.0 if table == 0 else -1.0
        scale = sign * 4.0 * math.pi * nrad / npts
        waves[0:ni, 0:npts] = x_ref[0]
        waves[ROW : ROW + ni, 0:npts] = x_ref[1]

        def wide_first(cols):
            return jnp.concatenate([first] * (cols // 128), axis=1)

        def density(k, _):
            at = pl.multiple_of(k * chunk, chunk)
            x = waves[:, pl.ds(at, chunk)]
            x1 = x.astype(bf16)
            x2 = (x - x1.astype(f32)).astype(bf16)
            right = jnp.concatenate([x1, x2, x1], axis=0)
            packed[0 : 4 * ROW, pl.ds(at, chunk)] = right[0 : 4 * ROW]
            mixed = jnp.dot(
                lhs32[:, 0 : 6 * ROW].astype(bf16), right, preferred_element_type=f32
            )
            pick = wide_first(chunk)
            value = jnp.where(
                pick,
                cores[2 * table : 2 * table + 1, pl.ds(at, chunk)],
                cores[2 * table + 1 : 2 * table + 2, pl.ds(at, chunk)],
            )
            for i in range(ni):
                own = jnp.where(pick, x[i : i + 1], x[ROW + i : ROW + i + 1])
                value = value + own * mixed[na * i : na * (i + 1)]
            rho[:, pl.ds(pl.multiple_of(at + 128, 128), chunk)] = value
            return 0

        lax.fori_loop(0, width // chunk, density, 0)

        def local(k, e_sum):
            at = pl.multiple_of(k * sub, sub)
            wide = rho[:, pl.ds(at, sub + 256)]
            n = wide[:, 128 : 128 + sub]
            after = pltpu.roll(wide, sub + 255, 1)[:, 128 : 128 + sub]
            before = pltpu.roll(wide, 1, 1)[:, 128 : 128 + sub]
            here = pl.ds(at, sub)
            weight = radial_ref[0:1, here]
            up, mid, down = radial_ref[1:2, here], radial_ref[2:3, here], radial_ref[3:4, here]
            slope = up * after + mid * n + down * before
            e, e_n, e_s = functional(n, slope * slope)
            weight = weight * scale
            we = e * weight
            for j in range(sub // 128):
                e_sum = e_sum + we[:, 128 * j : 128 * (j + 1)]
            part_n[:, here] = e_n * weight
            part_q[:, pl.ds(pl.multiple_of(at + 128, 128), sub)] = 2.0 * slope * e_s * weight
            return e_sum

        e_total = lax.fori_loop(0, width // sub, local, e_total)

        def back(k, _):
            at = pl.multiple_of(k * chunk, chunk)
            here = pl.ds(at, chunk)
            around = pl.ds(pl.multiple_of(at, 128), chunk + 256)
            wide = part_q[:, around]
            n_part = part_n[:, here]
            after = pltpu.roll(wide, chunk + 255, 1)[:, 128 : 128 + chunk]
            before = pltpu.roll(wide, 1, 1)[:, 128 : 128 + chunk]
            g = (
                n_part
                + radial_ref[5:6, here] * before
                + radial_ref[2:3, here] * wide[:, 128 : 128 + chunk]
                + radial_ref[6:7, here] * after
            )
            pick = wide_first(chunk)
            x = waves[:, here]
            for i in range(ni):
                own = jnp.where(pick, x[i : i + 1], x[ROW + i : ROW + i + 1]) * g
                hi = own.astype(bf16)
                grads[na * i : na * (i + 1), :] = hi
                grads[na * (ni + i) : na * (ni + i + 1), :] = (own - hi.astype(f32)).astype(bf16)
            out = lax.dot_general(
                grads[...], packed[0 : 4 * ROW, here], (((1,), (1,)), ((), ())),
                preferred_element_type=f32,
            )
            if table == 0:
                @pl.when(k == 0)
                def _():
                    total[...] = out

                @pl.when(k != 0)
                def _():
                    total[...] += out
            else:
                total[...] += out
            return 0

        lax.fori_loop(0, width // chunk, back, 0)

    tally = count_ref[0, 0]
    live = row < tally
    for i in range(ni):
        hi = total[na * i : na * (i + 1), :]
        lo = total[na * (ni + i) : na * (ni + i + 1), :]
        both = hi + lo
        value = both[:, 0 : 2 * ROW] + both[:, 2 * ROW : 4 * ROW]
        value = jnp.where(first[:, :ni], value[:, 0:ni], value[:, ROW : ROW + ni])
        h_ref[:, ni * i : ni * (i + 1)] = jnp.where(live[:, :ni], value, 0.0)
    energy = jnp.sum(e_total, axis=1, keepdims=True)
    energy = jnp.where(live[:, :1], energy, 0.0)
    diagonal = lax.broadcasted_iota(jnp.int32, (na, na), 0) == lax.broadcasted_iota(
        jnp.int32, (na, na), 1
    )
    e_ref[...] = jnp.sum(jnp.where(diagonal, energy, 0.0), axis=0, keepdims=True)


def atom_terms(count, species, matrices, ae, ps, ae_core, ps_core, chunk=2560, sub=1280):
    na, pairs = matrices.shape
    ni, npts = ae.shape[1], ae.shape[2]
    nrad = ae_core.shape[1]
    width = -(-npts // chunk) * chunk
    radial = radial_table(nrad, npts, width)
    radial[5] = np.roll(radial[1], 1)
    radial[6] = np.roll(radial[3], -1)
    vmem = pl.BlockSpec(memory_space=pltpu.VMEM)
    smem = pl.BlockSpec(memory_space=pltpu.SMEM)
    f32, bf16 = jnp.float32, jnp.bfloat16
    return pl.pallas_call(
        functools.partial(atoms_kernel, ni, nrad, npts, na, width, chunk, sub),
        out_shape=(
            jax.ShapeDtypeStruct((na, pairs), f32),
            jax.ShapeDtypeStruct((1, na), f32),
        ),
        in_specs=[smem, smem] + [vmem] * 6,
        out_specs=(vmem, vmem),
        scratch_shapes=[
            pltpu.VMEM((na * ni, 256), f32),
            pltpu.VMEM((2 * ROW, width), f32),
            pltpu.VMEM((4 * ROW, width), bf16),
            pltpu.VMEM((8, width), f32),
            pltpu.VMEM((na, width + 256), f32),
            pltpu.VMEM((na, width), f32),
            pltpu.VMEM((na, width + 256), f32),
            pltpu.VMEM((2 * na * ni, chunk), bf16),
            pltpu.VMEM((2 * na * ni, 4 * ROW), f32),
        ],
        compiler_params=pltpu.CompilerParams(vmem_limit_bytes=48 << 20),
        cost_estimate=pl.CostEstimate(
            flops=4 * na * ni * ni * npts * 2, transcendentals=na * npts * 10, bytes_accessed=3 << 20
        ),
        name="atoms",
    )(count, species, matrices, ae, ps, ae_core, ps_core, jnp.asarray(radial))


def upsampling(cells, halo):
    table = np.zeros((2 * cells + 4, cells + 2 * halo))
    for k in range(-2, 2 * cells + 2):
        i = k // 2
        table[k + 2, i + halo] = 0.75
        table[k + 2, i + halo + (1 if k % 2 else -1)] = 0.25
    return table


def grid_tables(nx, ny, nz):
    ux, uy, uz = upsampling(nx, 2), upsampling(ny, 2), upsampling(nz, 2)
    fx, fy, fz = 2 * nx, 2 * ny, 2 * nz

    def diff(u):
        return np.concatenate([np.zeros_like(u[:1]), u[2:] - u[:-2], np.zeros_like(u[:1])])

    places = [(-1, y) for y in range(fy)]
    places += [(x, y) for x in range(fx) for y in range(fy)]
    places += [(fx, y) for y in range(fy)]
    places += [(x, -1) for x in range(fx)] + [(x, fy) for x in range(fx)]

    def rows(wx, wy):
        return np.stack([np.outer(wy[y + 2], wx[x + 2]).reshape(-1) for x, y in places])

    left = np.concatenate([rows(ux, uy), rows(diff(ux), uy), rows(ux, diff(uy))])
    beyond = np.array([fz] + [fz // 2] * (fz - 2) + [-1])
    right = np.concatenate(
        [w[at + 2] for w in (uz, diff(uz)) for at in (np.arange(fz), beyond)]
    ).T
    return np.concatenate([left] * 3, axis=1), right


def split3(x):
    f32, bf16 = jnp.float32, jnp.bfloat16
    x1 = x.astype(bf16)
    rest = x - x1.astype(f32)
    x2 = rest.astype(bf16)
    return x1, x2, (rest - x2.astype(f32)).astype(bf16)


def grid_kernel(fx, fy, fz, c_ref, left_ref, right_ref, v_ref, e_ref):
    f32 = jnp.float32
    right = right_ref[...]
    parts = [jnp.dot(p, right, preferred_element_type=f32) for p in split3(c_ref[...])]
    lines = parts[0] + (parts[1] + parts[2])
    stack = jnp.concatenate(split3(lines), axis=0)
    inner = fx * fy
    rows = inner + 2 * fy + 2 * fx
    plane = jnp.dot(left_ref[...], stack[:, : 2 * fz], preferred_element_type=f32)
    dz_all = jnp.dot(left_ref[0:rows, :], stack[:, 2 * fz :], preferred_element_type=f32)
    inv = 0.5 / fine_step

    def fields(lo, hi, tile):
        cols = slice(fz * tile, fz * (tile + 1))
        n, dx, dy = (plane[rows * k + lo : rows * k + hi, cols] for k in range(3))
        dz = dz_all[lo:hi, cols]
        s = (inv * inv) * (dx * dx + dy * dy + dz * dz)
        return functional(n, s), dx, dy, dz

    main = slice(fy, fy + inner)
    (e, e_n, e_s), dx, dy, dz = fields(fy, fy + inner, 0)
    e_ref[...] = e.reshape(fx, fy, fz)
    (_, _, s_low), dx_low, _, _ = fields(0, fy, 0)
    (_, _, s_high), dx_high, _, _ = fields(fy + inner, 2 * fy + inner, 0)
    (_, _, s_side), _, dy_side, _ = fields(2 * fy + inner, rows, 0)
    (_, _, s_end), _, _, dz_end = fields(fy, fy + inner, 1)
    flux_x = jnp.concatenate([s_low * dx_low, e_s * dx, s_high * dx_high], axis=0)
    change = flux_x[2 * fy :] - flux_x[: inner]
    flux_z, end_z = e_s * dz, s_end * dz_end
    lane = lax.broadcasted_iota(jnp.int32, (inner, fz), 1)
    after = pltpu.roll(jnp.where(lane == 0, end_z, flux_z), fz - 1, 1)
    before = pltpu.roll(jnp.where(lane == fz - 1, end_z, flux_z), 1, 1)
    change = change + (after - before)
    flux_y, side_y = e_s * dy, s_side * dy_side
    line = lax.broadcasted_iota(jnp.int32, (fy, fz), 0)
    for x in range(fx):
        here = slice(fy * x, fy * (x + 1))
        own = flux_y[here]
        after = jnp.where(line == fy - 1, side_y[fx + x : fx + x + 1], pltpu.roll(own, fy - 1, 0))
        before = jnp.where(line == 0, side_y[x : x + 1], pltpu.roll(own, 1, 0))
        v_ref[x] = e_n[here] - (2.0 * inv * inv) * (change[here] + (after - before))


def grid_terms(columns, nx, ny, nz):
    left, right = grid_tables(nx, ny, nz)
    fx, fy, fz = 2 * nx, 2 * ny, 2 * nz
    vmem = pl.BlockSpec(memory_space=pltpu.VMEM)
    fine = jax.ShapeDtypeStruct((fx, fy, fz), jnp.float32)
    return pl.pallas_call(
        functools.partial(grid_kernel, fx, fy, fz),
        out_shape=(fine, fine),
        in_specs=[vmem] * 3,
        out_specs=(vmem, vmem),
        compiler_params=pltpu.CompilerParams(vmem_limit_bytes=32 << 20),
        cost_estimate=pl.CostEstimate(
            flops=300 * fx * fy * fz, transcendentals=10 * fx * fy * fz, bytes_accessed=2 << 20
        ),
        name="grid",
    )(columns, jnp.asarray(left, jnp.bfloat16), jnp.asarray(right, jnp.bfloat16))


def with_halo(cells, sides, width):
    for axis, dim in sides:
        count = lax.axis_size(axis)
        even = lax.axis_index(axis) % 2 == 0
        head = lax.slice_in_dim(cells, 0, width, axis=dim)
        tail = lax.slice_in_dim(cells, cells.shape[dim] - width, cells.shape[dim], axis=dim)
        inner = [(i, i ^ 1) for i in range(count)]
        outer = [(i, (i + 1 if i % 2 else i - 1) % count) for i in range(count)]
        first = lax.ppermute(jnp.where(even, tail, head), axis, inner)
        second = lax.ppermute(jnp.where(even, head, tail), axis, outer)
        cells = jnp.concatenate(
            [jnp.where(even, second, first), cells, jnp.where(even, first, second)], axis=dim
        )
    return cells


def shards(
    coarse_density,
    atom_count,
    atom_species,
    density_matrix,
    partial_waves,
    smooth_waves,
    core_density,
    smooth_core,
):
    rimmed = with_halo(coarse_density, (("gy", 1), ("gx", 0), ("gz", 2)), 2)
    columns = rimmed.transpose(1, 0, 2).reshape(-1, rimmed.shape[2])
    potential, energy_density = grid_terms(columns, *coarse_density.shape)
    slot_total, pair_total = density_matrix.shape[2:]
    placed, placed_energy = atom_terms(
        atom_count,
        atom_species,
        density_matrix.reshape(slot_total, pair_total),
        partial_waves,
        smooth_waves,
        core_density,
        smooth_core,
    )
    return (
        potential,
        energy_density,
        placed.reshape(density_matrix.shape),
        placed_energy.reshape(atom_species.shape),
    )


def solution(mesh):
    in_specs = (
        P("gx", "gy", "gz"),
        P("gx", ("gy", "gz")),
        P("gx", ("gy", "gz"), None),
        P("gx", ("gy", "gz"), None, None),
        P(),
        P(),
        P(),
        P(),
    )
    out_specs = (
        P("gx", "gy", "gz"),
        P("gx", "gy", "gz"),
        P("gx", ("gy", "gz"), None, None),
        P("gx", ("gy", "gz"), None),
    )
    return jax.shard_map(shards, mesh=mesh, in_specs=in_specs, out_specs=out_specs, check_vma=False)
```

```python
import functools
import math

import jax
import jax.numpy as jnp
import numpy as np
from jax import lax
from jax.experimental import pallas as pl
from jax.experimental.pallas import tpu as pltpu
from jax.sharding import PartitionSpec as P

fine_step = 0.1
sphere_radius = 2.5
enhance_kappa = 0.804
enhance_mu = 0.2195149727645171
gradient_beta = 0.06672455060314922
gradient_gamma = (1.0 - math.log(2.0)) / math.pi**2
perdew_amplitude = 0.031091
perdew_alpha = 0.2137
perdew_first = 7.5957
perdew_second = 3.5876
perdew_third = 1.6382
perdew_fourth = 0.49294

exchange_scale = -0.75 * (3.0 / math.pi) ** (1.0 / 3.0)
fermi_scale = (3.0 * math.pi**2) ** (1.0 / 3.0)
radius_scale = (3.0 / (4.0 * math.pi)) ** (1.0 / 3.0)
reduced_scale = 1.0 / (4.0 * fermi_scale**2)
scaled_scale = math.pi / (16.0 * fermi_scale)
beta_ratio = gradient_beta / gradient_gamma
fit = [
    2.0 * perdew_amplitude * c * radius_scale ** (k / 2.0)
    for k, c in ((1, perdew_first), (2, perdew_second), (3, perdew_third), (4, perdew_fourth))
]
ln2 = math.log(2.0)
third = perdew_amplitude / 3.0


def functional(n, s):
    m = jnp.exp2(jnp.log2(n) * (-1.0 / 6.0))
    m2 = m * m
    m4 = m2 * m2
    m8 = m4 * m4
    by_p = (enhance_mu / enhance_kappa * reduced_scale) * (m8 * m8)
    by_t = (beta_ratio * scaled_scale) * (m8 * m4 * m2)
    fitted = m * (fit[0] + m * (fit[1] + m * (fit[2] + m * fit[3])))
    slope = m * (
        third * fit[0]
        + m * (2.0 * third * fit[1] + m * (3.0 * third * fit[2] + m * (4.0 * third * fit[3])))
    )
    one_fit = 1.0 + fitted
    enhance = 1.0 + s * by_p
    fit_both = fitted * one_fit
    joint = 1.0 / (fit_both * enhance)
    inverse_fit = joint * enhance
    damp = joint * fit_both
    log_term = jnp.log2(1.0 + one_fit * inverse_fit)
    alpha_r = (perdew_alpha * radius_scale) * m2
    one_alpha = 1.0 + alpha_r
    product_c = one_alpha * log_term
    inv_exp = 1.0 / (jnp.exp2((2.0 * perdew_amplitude / gradient_gamma) * product_c) - 1.0)
    c_n = (2.0 * ln2 * third) * (alpha_r * log_term) - one_alpha * (slope * inverse_fit)
    t = s * by_t
    q = t * inv_exp
    num = 1.0 + q
    den_inv = 1.0 / (1.0 + q * num)
    z = 1.0 + t * (num * den_inv)
    z_inv = 1.0 / z
    den_z = den_inv * z_inv
    h_t = ((num + q) * den_inv) * den_z
    h_c = (t * (q * den_inv)) * ((q * (1.0 + num)) * den_z) * (1.0 + inv_exp)
    ch = (gradient_gamma * ln2) * jnp.log2(z) - (2.0 * perdew_amplitude * ln2) * product_c
    x = (enhance_kappa * exchange_scale) * (n * m4)
    xf = x * ((1.0 + 1.0 / enhance_kappa) - damp)
    xd = x * damp
    e = n * (xf + ch)
    e_n = (
        (4.0 / 3.0) * xf
        + (8.0 / 3.0) * (xd * (damp - 1.0))
        + ch
        + (c_n - h_c * c_n)
        - (7.0 / 3.0 * gradient_gamma) * (h_t * t)
    )
    e_s = n * ((xd * damp) * by_p + gradient_gamma * (h_t * by_t))
    return e, e_n, e_s


ROW = 24


def radial_table(nrad, npts, width):
    g = np.arange(width) % nrad
    live = np.arange(width) < npts
    r = sphere_radius * (g + 0.5) / nrad
    w = r * r * (sphere_radius / nrad)
    k = nrad / sphere_radius
    up = np.where(g == nrad - 1, 0.0, np.where(g == 0, k, 0.5 * k))
    down = np.where(g == 0, 0.0, np.where(g == nrad - 1, -k, -0.5 * k))
    mid = np.where(g == 0, -k, np.where(g == nrad - 1, k, 0.0))
    rows = np.stack([w, up, mid, down] + [np.zeros(width)] * 4) * live
    return rows.astype(np.float32)


def atoms_kernel(
    ni, nrad, npts, na, units,
    count_ref, species_ref, d_ref, ae_ref, ps_ref, ae_core_ref, ps_core_ref, radial_ref,
    h_in_ref, e_in_ref, h_ref, e_ref,
    lhs32, cores, total, *scratch,
):
    f32, bf16 = jnp.float32, jnp.bfloat16
    row = lax.broadcasted_iota(jnp.int32, (na, 128), 0)
    species = jnp.zeros((na, 128), jnp.int32)
    for a in range(na):
        species = jnp.where(row == a, species_ref[0, 0, a], species)
    first = species == 0
    first_f = jnp.where(first, 1.0, 0.0).astype(f32)
    second_f = 1.0 - first_f

    lhs32[...] = jnp.zeros_like(lhs32)
    for i in range(ni):
        d = d_ref[:, ni * i : ni * (i + 1)]
        d1 = d.astype(bf16).astype(f32)
        d2 = d - d1
        here = pl.ds(na * i, na)
        for block, part in ((0, d1), (1, d1), (2, d2)):
            at = 2 * ROW * block
            lhs32[here, at : at + ni] = part * first_f[:, :ni]
            lhs32[here, at + ROW : at + ROW + ni] = part * second_f[:, :ni]
    lhs = lhs32[:, 0 : 6 * ROW].astype(bf16)

    longest = max(high - low for _, low, high in units)
    cores[0:2, 0:nrad] = ae_core_ref[...]
    cores[2:4, 0:nrad] = ps_core_ref[...]
    reach = nrad
    while reach < longest:
        more = min(reach, longest - reach)
        cores[0:4, reach : reach + more] = cores[0:4, 0:more]
        reach += more

    e_sum = jnp.zeros((na, 128), f32)
    for u, (table, low, high) in enumerate(units):
        waves, packed, rho, part_q = scratch[4 * u : 4 * u + 4]
        x_ref = (ae_ref, ps_ref)[table]
        size, live = high - low, min(high, npts) - low
        tail = live // 128 * 128
        if tail < size:
            waves[:, tail:] = jnp.zeros((2 * ROW, size - tail), f32)
        for s in range(2):
            waves[ROW * s + 16 : ROW * (s + 1), 0:tail] = jnp.zeros((ROW - 16, tail), f32)
            waves[ROW * s : ROW * s + ni, 0:live] = x_ref[s, :, low : low + live]
        pick = jnp.concatenate([first] * (size // 128), axis=1)

        x = waves[...]
        x1 = x.astype(bf16)
        x2 = (x - x1.astype(f32)).astype(bf16)
        packed[...] = jnp.concatenate([x1, x2], axis=0)
        mixed = jnp.dot(lhs, jnp.concatenate([x1, x2, x1], axis=0), preferred_element_type=f32)
        n = jnp.where(
            pick,
            cores[2 * table : 2 * table + 1, 0:size],
            cores[2 * table + 1 : 2 * table + 2, 0:size],
        )
        for i in range(ni):
            own = jnp.where(pick, x[i : i + 1], x[ROW + i : ROW + i + 1])
            n = n + own * mixed[na * i : na * (i + 1)]
        rho[...] = n

        scale = (-1.0 if table else 1.0) * 4.0 * math.pi * nrad / npts
        n = rho[...]
        radial = radial_ref[:, low:high]
        weight = radial[0:1] * scale
        up, mid, down = radial[1:2], radial[2:3], radial[3:4]
        slope = up * pltpu.roll(n, size - 1, 1) + mid * n + down * pltpu.roll(n, 1, 1)
        e, e_n, e_s = functional(n, slope * slope)
        we = e * weight
        for j in range(size // 128):
            e_sum = e_sum + we[:, 128 * j : 128 * (j + 1)]
        part_q[...] = (slope * e_s) * (2.0 * weight)
        q = part_q[...]
        g = e_n * weight + mid * q
        g = g + radial[5:6] * pltpu.roll(q, 1, 1) + radial[6:7] * pltpu.roll(q, size - 1, 1)
        rho[...] = g
        g = rho[...]
        x = waves[...]
        hi, lo = [], []
        for i in range(ni):
            own = jnp.where(pick, x[i : i + 1], x[ROW + i : ROW + i + 1]) * g
            top = own.astype(bf16)
            hi.append(top)
            lo.append((own - top.astype(f32)).astype(bf16))
        out = lax.dot_general(
            jnp.concatenate(hi + lo, axis=0), packed[...], (((1,), (1,)), ((), ())),
            preferred_element_type=f32,
        )
        if u == 0:
            total[...] = out
        else:
            total[...] += out

    tally = count_ref[0, 0]
    live = row < tally
    for i in range(ni):
        both = total[na * i : na * (i + 1), :] + total[na * (ni + i) : na * (ni + i + 1), :]
        value = both[:, 0 : 2 * ROW] + both[:, 2 * ROW : 4 * ROW]
        value = jnp.where(first[:, :ni], value[:, 0:ni], value[:, ROW : ROW + ni])
        here = slice(ni * i, ni * (i + 1))
        h_ref[:, here] = h_in_ref[:, here] + jnp.where(live[:, :ni], value, 0.0)
    energy = jnp.sum(e_sum, axis=1, keepdims=True)
    energy = jnp.where(live[:, :1], energy, 0.0)
    diagonal = lax.broadcasted_iota(jnp.int32, (na, na), 0) == lax.broadcasted_iota(
        jnp.int32, (na, na), 1
    )
    e_ref[...] = e_in_ref[...] + jnp.sum(jnp.where(diagonal, energy, 0.0), axis=0, keepdims=True)


def atom_terms(units, sums, count, species, matrices, ae, ps, ae_core, ps_core):
    na, pairs = matrices.shape
    ni, npts = ae.shape[1], ae.shape[2]
    nrad = ae_core.shape[1]
    width = -(-npts // 128) * 128
    radial = radial_table(nrad, npts, width)
    radial[5] = np.roll(radial[1], 1)
    radial[6] = np.roll(radial[3], -1)
    vmem = pl.BlockSpec(memory_space=pltpu.VMEM)
    smem = pl.BlockSpec(memory_space=pltpu.SMEM)
    f32, bf16 = jnp.float32, jnp.bfloat16
    points = sum(high - low for _, low, high in units)
    scratch = [
        pltpu.VMEM((na * ni, 256), f32),
        pltpu.VMEM((8, max(high - low for _, low, high in units)), f32),
        pltpu.VMEM((2 * na * ni, 4 * ROW), f32),
    ]
    for _, low, high in units:
        scratch += [
            pltpu.VMEM((2 * ROW, high - low), f32),
            pltpu.VMEM((4 * ROW, high - low), bf16),
            pltpu.VMEM((na, high - low), f32),
            pltpu.VMEM((na, high - low), f32),
        ]
    return pl.pallas_call(
        functools.partial(atoms_kernel, ni, nrad, npts, na, units),
        out_shape=(
            jax.ShapeDtypeStruct((na, pairs), f32),
            jax.ShapeDtypeStruct((1, na), f32),
        ),
        in_specs=[smem, smem] + [vmem] * 8,
        out_specs=(vmem, vmem),
        scratch_shapes=scratch,
        compiler_params=pltpu.CompilerParams(vmem_limit_bytes=40 << 20),
        cost_estimate=pl.CostEstimate(
            flops=4 * na * ni * ni * points, transcendentals=na * points * 10, bytes_accessed=2 << 20
        ),
        name="atoms",
    )(count, species, matrices, ae, ps, ae_core, ps_core, jnp.asarray(radial), *sums)


def upsampling(cells, halo):
    table = np.zeros((2 * cells + 4, cells + 2 * halo))
    for k in range(-2, 2 * cells + 2):
        i = k // 2
        table[k + 2, i + halo] = 0.75
        table[k + 2, i + halo + (1 if k % 2 else -1)] = 0.25
    return table


def grid_tables(nx, ny, nz):
    ux, uy, uz = upsampling(nx, 2), upsampling(ny, 2), upsampling(nz, 2)
    fx, fy, fz = 2 * nx, 2 * ny, 2 * nz

    def diff(u):
        return np.concatenate([np.zeros_like(u[:1]), u[2:] - u[:-2], np.zeros_like(u[:1])])

    places = [(-1, y) for y in range(fy)]
    places += [(x, y) for x in range(fx) for y in range(fy)]
    places += [(fx, y) for y in range(fy)]
    places += [(x, -1) for x in range(fx)] + [(x, fy) for x in range(fx)]

    def rows(wx, wy):
        return np.stack([np.outer(wy[y + 2], wx[x + 2]).reshape(-1) for x, y in places])

    left = np.concatenate([rows(ux, uy), rows(diff(ux), uy), rows(ux, diff(uy))])
    beyond = np.array([fz] + [fz // 2] * (fz - 2) + [-1])
    right = np.concatenate(
        [w[at + 2] for w in (uz, diff(uz)) for at in (np.arange(fz), beyond)]
    ).T
    return np.concatenate([left] * 3, axis=1), right


def split3(x):
    f32, bf16 = jnp.float32, jnp.bfloat16
    x1 = x.astype(bf16)
    rest = x - x1.astype(f32)
    x2 = rest.astype(bf16)
    return x1, x2, (rest - x2.astype(f32)).astype(bf16)


def grid_kernel(fx, fy, fz, c_ref, left_ref, right_ref, v_ref, e_ref):
    f32 = jnp.float32
    right = right_ref[...]
    parts = [jnp.dot(p, right, preferred_element_type=f32) for p in split3(c_ref[...])]
    lines = parts[0] + (parts[1] + parts[2])
    stack = jnp.concatenate(split3(lines), axis=0)
    inner = fx * fy
    rows = inner + 2 * fy + 2 * fx
    plane = jnp.dot(left_ref[...], stack[:, : 2 * fz], preferred_element_type=f32)
    dz_all = jnp.dot(left_ref[0:rows, :], stack[:, 2 * fz :], preferred_element_type=f32)
    inv = 0.5 / fine_step

    def fields(lo, hi, tile):
        cols = slice(fz * tile, fz * (tile + 1))
        n, dx, dy = (plane[rows * k + lo : rows * k + hi, cols] for k in range(3))
        dz = dz_all[lo:hi, cols]
        s = (inv * inv) * (dx * dx + dy * dy + dz * dz)
        return functional(n, s), dx, dy, dz

    main = slice(fy, fy + inner)
    (e, e_n, e_s), dx, dy, dz = fields(fy, fy + inner, 0)
    e_ref[...] = e.reshape(fx, fy, fz)
    (_, _, s_low), dx_low, _, _ = fields(0, fy, 0)
    (_, _, s_high), dx_high, _, _ = fields(fy + inner, 2 * fy + inner, 0)
    (_, _, s_side), _, dy_side, _ = fields(2 * fy + inner, rows, 0)
    (_, _, s_end), _, _, dz_end = fields(fy, fy + inner, 1)
    flux_x = jnp.concatenate([s_low * dx_low, e_s * dx, s_high * dx_high], axis=0)
    change = flux_x[2 * fy :] - flux_x[: inner]
    flux_z, end_z = e_s * dz, s_end * dz_end
    lane = lax.broadcasted_iota(jnp.int32, (inner, fz), 1)
    after = pltpu.roll(jnp.where(lane == 0, end_z, flux_z), fz - 1, 1)
    before = pltpu.roll(jnp.where(lane == fz - 1, end_z, flux_z), 1, 1)
    change = change + (after - before)
    flux_y, side_y = e_s * dy, s_side * dy_side
    line = lax.broadcasted_iota(jnp.int32, (fy, fz), 0)
    for x in range(fx):
        here = slice(fy * x, fy * (x + 1))
        own = flux_y[here]
        after = jnp.where(line == fy - 1, side_y[fx + x : fx + x + 1], pltpu.roll(own, fy - 1, 0))
        before = jnp.where(line == 0, side_y[x : x + 1], pltpu.roll(own, 1, 0))
        v_ref[x] = e_n[here] - (2.0 * inv * inv) * (change[here] + (after - before))


def grid_terms(columns, nx, ny, nz):
    left, right = grid_tables(nx, ny, nz)
    fx, fy, fz = 2 * nx, 2 * ny, 2 * nz
    vmem = pl.BlockSpec(memory_space=pltpu.VMEM)
    fine = jax.ShapeDtypeStruct((fx, fy, fz), jnp.float32)
    return pl.pallas_call(
        functools.partial(grid_kernel, fx, fy, fz),
        out_shape=(fine, fine),
        in_specs=[vmem] * 3,
        out_specs=(vmem, vmem),
        compiler_params=pltpu.CompilerParams(vmem_limit_bytes=32 << 20),
        cost_estimate=pl.CostEstimate(
            flops=300 * fx * fy * fz, transcendentals=10 * fx * fy * fz, bytes_accessed=2 << 20
        ),
        name="grid",
    )(columns, jnp.asarray(left, jnp.bfloat16), jnp.asarray(right, jnp.bfloat16))


def with_halo(cells, axis, dim, width, work, sums):
    count = lax.axis_size(axis)
    even = lax.axis_index(axis) % 2 == 0
    head = lax.slice_in_dim(cells, 0, width, axis=dim)
    tail = lax.slice_in_dim(cells, cells.shape[dim] - width, cells.shape[dim], axis=dim)
    inner = [(i, i ^ 1) for i in range(count)]
    outer = [(i, (i + 1 if i % 2 else i - 1) % count) for i in range(count)]
    first = lax.ppermute(jnp.where(even, tail, head), axis, inner)
    second = lax.ppermute(jnp.where(even, head, tail), axis, outer)
    sums = work(sums)
    first, second, sums = lax.optimization_barrier((first, second, sums))
    return (
        jnp.concatenate(
            [jnp.where(even, second, first), cells, jnp.where(even, first, second)], axis=dim
        ),
        sums,
    )


def shards(
    coarse_density,
    atom_count,
    atom_species,
    density_matrix,
    partial_waves,
    smooth_waves,
    core_density,
    smooth_core,
):
    slots, pairs = density_matrix.shape[2:]
    owned = (
        atom_count,
        atom_species,
        density_matrix.reshape(slots, pairs),
        partial_waves,
        smooth_waves,
        core_density,
        smooth_core,
    )
    sums = (jnp.zeros((slots, pairs), jnp.float32), jnp.zeros((1, slots), jnp.float32))
    cells = coarse_density
    runs = [(), ((0, 0, 3200), (0, 3200, 5120)), ((1, 0, 3200), (1, 3200, 5120))]
    for (axis, dim), units in zip((("gy", 1), ("gx", 0), ("gz", 2)), runs):
        cells, sums = with_halo(
            cells, axis, dim, 2, lambda s: atom_terms(units, s, *owned) if units else s, sums
        )
    placed, placed_energy = sums
    columns = cells.transpose(1, 0, 2).reshape(-1, cells.shape[2])
    potential, energy_density = grid_terms(columns, *coarse_density.shape)
    return (
        potential,
        energy_density,
        placed.reshape(density_matrix.shape),
        placed_energy.reshape(atom_species.shape),
    )


def solution(mesh):
    in_specs = (
        P("gx", "gy", "gz"),
        P("gx", ("gy", "gz")),
        P("gx", ("gy", "gz"), None),
        P("gx", ("gy", "gz"), None, None),
        P(),
        P(),
        P(),
        P(),
    )
    out_specs = (
        P("gx", "gy", "gz"),
        P("gx", "gy", "gz"),
        P("gx", ("gy", "gz"), None, None),
        P("gx", ("gy", "gz"), None),
    )
    return jax.shard_map(shards, mesh=mesh, in_specs=in_specs, out_specs=out_specs, check_vma=False)
```

```python
import functools
import math

import jax
import jax.numpy as jnp
import numpy as np
from jax import lax
from jax.experimental import pallas as pl
from jax.experimental.pallas import tpu as pltpu
from jax.sharding import PartitionSpec as P

fine_step = 0.1
sphere_radius = 2.5
enhance_kappa = 0.804
enhance_mu = 0.2195149727645171
gradient_beta = 0.06672455060314922
gradient_gamma = (1.0 - math.log(2.0)) / math.pi**2
perdew_amplitude = 0.031091
perdew_alpha = 0.2137
perdew_first = 7.5957
perdew_second = 3.5876
perdew_third = 1.6382
perdew_fourth = 0.49294

exchange_scale = -0.75 * (3.0 / math.pi) ** (1.0 / 3.0)
fermi_scale = (3.0 * math.pi**2) ** (1.0 / 3.0)
radius_scale = (3.0 / (4.0 * math.pi)) ** (1.0 / 3.0)
reduced_scale = 1.0 / (4.0 * fermi_scale**2)
scaled_scale = math.pi / (16.0 * fermi_scale)
beta_ratio = gradient_beta / gradient_gamma
fit = [
    2.0 * perdew_amplitude * c * radius_scale ** (k / 2.0)
    for k, c in ((1, perdew_first), (2, perdew_second), (3, perdew_third), (4, perdew_fourth))
]
ln2 = math.log(2.0)
third = perdew_amplitude / 3.0


def functional(n, s):
    m = jnp.exp2(jnp.log2(n) * (-1.0 / 6.0))
    m2 = m * m
    m4 = m2 * m2
    m8 = m4 * m4
    by_p = (enhance_mu / enhance_kappa * reduced_scale) * (m8 * m8)
    by_t = (beta_ratio * scaled_scale) * (m8 * m4 * m2)
    fitted = m * (fit[0] + m * (fit[1] + m * (fit[2] + m * fit[3])))
    slope = m * (
        third * fit[0]
        + m * (2.0 * third * fit[1] + m * (3.0 * third * fit[2] + m * (4.0 * third * fit[3])))
    )
    one_fit = 1.0 + fitted
    enhance = 1.0 + s * by_p
    fit_both = fitted * one_fit
    joint = 1.0 / (fit_both * enhance)
    inverse_fit = joint * enhance
    damp = joint * fit_both
    log_term = jnp.log2(1.0 + one_fit * inverse_fit)
    alpha_r = (perdew_alpha * radius_scale) * m2
    one_alpha = 1.0 + alpha_r
    product_c = one_alpha * log_term
    inv_exp = 1.0 / (jnp.exp2((2.0 * perdew_amplitude / gradient_gamma) * product_c) - 1.0)
    c_n = (2.0 * ln2 * third) * (alpha_r * log_term) - one_alpha * (slope * inverse_fit)
    t = s * by_t
    q = t * inv_exp
    num = 1.0 + q
    den_inv = 1.0 / (1.0 + q * num)
    z = 1.0 + t * (num * den_inv)
    z_inv = 1.0 / z
    den_z = den_inv * z_inv
    h_t = ((num + q) * den_inv) * den_z
    h_c = (t * (q * den_inv)) * ((q * (1.0 + num)) * den_z) * (1.0 + inv_exp)
    ch = (gradient_gamma * ln2) * jnp.log2(z) - (2.0 * perdew_amplitude * ln2) * product_c
    x = (enhance_kappa * exchange_scale) * (n * m4)
    xf = x * ((1.0 + 1.0 / enhance_kappa) - damp)
    xd = x * damp
    e = n * (xf + ch)
    e_n = (
        (4.0 / 3.0) * xf
        + (8.0 / 3.0) * (xd * (damp - 1.0))
        + ch
        + (c_n - h_c * c_n)
        - (7.0 / 3.0 * gradient_gamma) * (h_t * t)
    )
    e_s = n * ((xd * damp) * by_p + gradient_gamma * (h_t * by_t))
    return e, e_n, e_s


ROW = 24


RADIAL = 8


def radial_table(nrad):
    g = np.arange(nrad)
    r = sphere_radius * (g + 0.5) / nrad
    k = nrad / sphere_radius
    up = np.where(g == nrad - 1, 0.0, np.where(g == 0, k, 0.5 * k))
    down = np.where(g == 0, 0.0, np.where(g == nrad - 1, -k, -0.5 * k))
    mid = np.where(g == 0, -k, np.where(g == nrad - 1, k, 0.0))
    rows = [r * r * (sphere_radius / nrad), up, mid, down, np.roll(up, 1), np.roll(down, -1)]
    return np.stack(rows + [np.zeros(nrad)] * 2).astype(np.float32)


def first_species(species_ref, na):
    row = lax.broadcasted_iota(jnp.int32, (na, 128), 0)
    species = jnp.zeros((na, 128), jnp.int32)
    for a in range(na):
        species = jnp.where(row == a, species_ref[0, 0, a], species)
    return species == 0


def prepare_kernel(
    ni, nrad, npts, na,
    species_ref, d_ref, ae_core_ref, ps_core_ref, radial_ref, lhs_ref, line_ref, lhs32,
):
    f32, bf16 = jnp.float32, jnp.bfloat16
    first_f = jnp.where(first_species(species_ref, na), 1.0, 0.0).astype(f32)
    second_f = 1.0 - first_f
    lhs32[...] = jnp.zeros_like(lhs32)
    for i in range(ni):
        d = d_ref[:, ni * i : ni * (i + 1)]
        d1 = d.astype(bf16).astype(f32)
        d2 = d - d1
        here = pl.ds(na * i, na)
        for block, part in ((0, d1), (1, d1), (2, d2)):
            at = 2 * ROW * block
            lhs32[here, at : at + ni] = part * first_f[:, :ni]
            lhs32[here, at + ROW : at + ROW + ni] = part * second_f[:, :ni]
    lhs_ref[...] = lhs32[:, 0 : 6 * ROW].astype(bf16)

    width = line_ref.shape[1]
    line_ref[0:2, 0:nrad] = ae_core_ref[...]
    line_ref[2:4, 0:nrad] = ps_core_ref[...]
    line_ref[4:RADIAL, 0:nrad] = jnp.ones((RADIAL - 4, nrad), f32)
    line_ref[RADIAL:, 0:nrad] = radial_ref[...]
    reach = nrad
    while reach < width:
        more = min(reach, width - reach)
        line_ref[:, reach : reach + more] = line_ref[:, 0:more]
        reach += more
    line_ref[RADIAL:, npts:] = jnp.zeros((8, width - npts), f32)


def prepare(species, matrices, ae_core, ps_core, npts):
    na, pairs = matrices.shape
    ni = math.isqrt(pairs)
    nrad = ae_core.shape[1]
    width = -(-npts // 128) * 128
    vmem = pl.BlockSpec(memory_space=pltpu.VMEM)
    smem = pl.BlockSpec(memory_space=pltpu.SMEM)
    f32, bf16 = jnp.float32, jnp.bfloat16
    return pl.pallas_call(
        functools.partial(prepare_kernel, ni, nrad, npts, na),
        out_shape=(
            jax.ShapeDtypeStruct((na * ni, 6 * ROW), bf16),
            jax.ShapeDtypeStruct((RADIAL + 8, width), f32),
        ),
        in_specs=[smem] + [vmem] * 4,
        out_specs=(vmem,) * 2,
        scratch_shapes=[pltpu.VMEM((na * ni, 256), f32)],
        compiler_params=pltpu.CompilerParams(vmem_limit_bytes=8 << 20),
        cost_estimate=pl.CostEstimate(flops=1 << 31, transcendentals=0, bytes_accessed=6 << 20),
        name="prepare",
    )(species, matrices, ae_core, ps_core, jnp.asarray(radial_table(nrad)))


def atoms_kernel(
    ni, nrad, npts, na, table, runs, has_sums, carried,
    count_ref, species_ref, x_ref, lhs_ref, line_ref, *refs,
):
    f32, bf16 = jnp.float32, jnp.bfloat16
    if has_sums:
        h_in_ref, e_in_ref, *refs = refs
    carry_in, (h_ref, e_ref, *refs) = refs[:carried], refs[carried:]
    carry_out, (total, *scratch) = refs[:carried], refs[carried:]
    for source, target in zip(carry_in, carry_out):
        target[...] = source[...]
    first = first_species(species_ref, na)
    row = lax.broadcasted_iota(jnp.int32, (na, 128), 0)

    e_sum = jnp.zeros((na, 128), f32)
    for u, (low, high) in enumerate(runs):
        waves, packed, rho, part_q = scratch[4 * u : 4 * u + 4]
        size, live = high - low, min(high, npts) - low
        tail = live // 128 * 128
        if tail < size:
            waves[:, tail:] = jnp.zeros((2 * ROW, size - tail), f32)
        for s in range(2):
            waves[ROW * s + 16 : ROW * (s + 1), 0:tail] = jnp.zeros((ROW - 16, tail), f32)
            waves[ROW * s : ROW * s + ni, 0:live] = x_ref[s, :, low : low + live]
        pick = jnp.concatenate([first] * (size // 128), axis=1)

        x = waves[...]
        x1 = x.astype(bf16)
        x2 = (x - x1.astype(f32)).astype(bf16)
        packed[...] = jnp.concatenate([x1, x2], axis=0)
        mixed = jnp.dot(
            lhs_ref[...], jnp.concatenate([x1, x2, x1], axis=0), preferred_element_type=f32
        )
        n = jnp.where(
            pick,
            line_ref[2 * table : 2 * table + 1, low:high],
            line_ref[2 * table + 1 : 2 * table + 2, low:high],
        )
        for i in range(ni):
            own = jnp.where(pick, x[i : i + 1], x[ROW + i : ROW + i + 1])
            n = n + own * mixed[na * i : na * (i + 1)]
        rho[...] = n

        scale = (-1.0 if table else 1.0) * 4.0 * math.pi * nrad / npts
        n = rho[...]
        radial = line_ref[RADIAL:, low:high]
        weight = radial[0:1] * scale
        up, mid, down = radial[1:2], radial[2:3], radial[3:4]
        slope = up * pltpu.roll(n, size - 1, 1) + mid * n + down * pltpu.roll(n, 1, 1)
        e, e_n, e_s = functional(n, slope * slope)
        we = e * weight
        for j in range(size // 128):
            e_sum = e_sum + we[:, 128 * j : 128 * (j + 1)]
        part_q[...] = (slope * e_s) * (2.0 * weight)
        q = part_q[...]
        g = e_n * weight + mid * q
        g = g + radial[4:5] * pltpu.roll(q, 1, 1) + radial[5:6] * pltpu.roll(q, size - 1, 1)
        rho[...] = g
        g = rho[...]
        x = waves[...]
        hi, lo = [], []
        for i in range(ni):
            own = jnp.where(pick, x[i : i + 1], x[ROW + i : ROW + i + 1]) * g
            top = own.astype(bf16)
            hi.append(top)
            lo.append((own - top.astype(f32)).astype(bf16))
        out = lax.dot_general(
            jnp.concatenate(hi + lo, axis=0), packed[...], (((1,), (1,)), ((), ())),
            preferred_element_type=f32,
        )
        if u == 0:
            total[...] = out
        else:
            total[...] += out

    tally = count_ref[0, 0]
    live = row < tally
    for i in range(ni):
        both = total[na * i : na * (i + 1), :] + total[na * (ni + i) : na * (ni + i + 1), :]
        value = both[:, 0 : 2 * ROW] + both[:, 2 * ROW : 4 * ROW]
        value = jnp.where(first[:, :ni], value[:, 0:ni], value[:, ROW : ROW + ni])
        here = slice(ni * i, ni * (i + 1))
        value = jnp.where(live[:, :ni], value, 0.0)
        h_ref[:, here] = h_in_ref[:, here] + value if has_sums else value
    energy = jnp.sum(e_sum, axis=1, keepdims=True)
    energy = jnp.where(live[:, :1], energy, 0.0)
    diagonal = lax.broadcasted_iota(jnp.int32, (na, na), 0) == lax.broadcasted_iota(
        jnp.int32, (na, na), 1
    )
    energy = jnp.sum(jnp.where(diagonal, energy, 0.0), axis=0, keepdims=True)
    e_ref[...] = e_in_ref[...] + energy if has_sums else energy


def atom_terms(table, count, species, x, lhs, line, nrad, sums=(), carry=()):
    _, ni, npts = x.shape
    na = lhs.shape[0] // ni
    width = line.shape[1]
    cut = math.lcm(nrad, 128)
    runs = [(low, min(low + cut, width)) for low in range(0, width, cut)]
    vmem = pl.BlockSpec(memory_space=pltpu.VMEM)
    smem = pl.BlockSpec(memory_space=pltpu.SMEM)
    f32, bf16 = jnp.float32, jnp.bfloat16
    scratch = [pltpu.VMEM((2 * na * ni, 4 * ROW), f32)]
    for low, high in runs:
        scratch += [
            pltpu.VMEM((2 * ROW, high - low), f32),
            pltpu.VMEM((4 * ROW, high - low), bf16),
            pltpu.VMEM((na, high - low), f32),
            pltpu.VMEM((na, high - low), f32),
        ]
    return pl.pallas_call(
        functools.partial(atoms_kernel, ni, nrad, npts, na, table, runs, bool(sums), len(carry)),
        out_shape=(
            jax.ShapeDtypeStruct((na, ni * ni), f32),
            jax.ShapeDtypeStruct((1, na), f32),
            *(jax.ShapeDtypeStruct(c.shape, c.dtype) for c in carry),
        ),
        in_specs=[smem, smem] + [vmem] * (3 + len(sums) + len(carry)),
        out_specs=(vmem,) * (2 + len(carry)),
        scratch_shapes=scratch,
        compiler_params=pltpu.CompilerParams(vmem_limit_bytes=32 << 20),
        cost_estimate=pl.CostEstimate(
            flops=4 * na * ni * ni * npts, transcendentals=na * npts * 10, bytes_accessed=2 << 20
        ),
        name="atoms",
    )(count, species, x, lhs, line, *sums, *carry)


def upsampling(cells, halo):
    table = np.zeros((2 * cells + 4, cells + 2 * halo))
    for k in range(-2, 2 * cells + 2):
        i = k // 2
        table[k + 2, i + halo] = 0.75
        table[k + 2, i + halo + (1 if k % 2 else -1)] = 0.25
    return table


def grid_tables(nx, ny, nz):
    ux, uy, uz = upsampling(nx, 2), upsampling(ny, 2), upsampling(nz, 2)
    fx, fy, fz = 2 * nx, 2 * ny, 2 * nz

    def diff(u):
        return np.concatenate([np.zeros_like(u[:1]), u[2:] - u[:-2], np.zeros_like(u[:1])])

    places = [(-1, y) for y in range(fy)]
    places += [(x, y) for x in range(fx) for y in range(fy)]
    places += [(fx, y) for y in range(fy)]
    places += [(x, -1) for x in range(fx)] + [(x, fy) for x in range(fx)]

    def rows(wx, wy):
        return np.stack([np.outer(wy[y + 2], wx[x + 2]).reshape(-1) for x, y in places])

    left = np.concatenate([rows(ux, uy), rows(diff(ux), uy), rows(ux, diff(uy))])
    beyond = np.array([fz] + [fz // 2] * (fz - 2) + [-1])
    right = np.concatenate(
        [w[at + 2] for w in (uz, diff(uz)) for at in (np.arange(fz), beyond)]
    ).T
    return np.concatenate([left] * 3, axis=1), right


def split3(x):
    f32, bf16 = jnp.float32, jnp.bfloat16
    x1 = x.astype(bf16)
    rest = x - x1.astype(f32)
    x2 = rest.astype(bf16)
    return x1, x2, (rest - x2.astype(f32)).astype(bf16)


def grid_kernel(fx, fy, fz, c_ref, left_ref, right_ref, v_ref, e_ref):
    f32 = jnp.float32
    right = right_ref[...]
    parts = [jnp.dot(p, right, preferred_element_type=f32) for p in split3(c_ref[...])]
    lines = parts[0] + (parts[1] + parts[2])
    stack = jnp.concatenate(split3(lines), axis=0)
    inner = fx * fy
    rows = inner + 2 * fy + 2 * fx
    plane = jnp.dot(left_ref[...], stack[:, : 2 * fz], preferred_element_type=f32)
    dz_all = jnp.dot(left_ref[0:rows, :], stack[:, 2 * fz :], preferred_element_type=f32)
    inv = 0.5 / fine_step

    def fields(lo, hi, tile):
        cols = slice(fz * tile, fz * (tile + 1))
        n, dx, dy = (plane[rows * k + lo : rows * k + hi, cols] for k in range(3))
        dz = dz_all[lo:hi, cols]
        s = (inv * inv) * (dx * dx + dy * dy + dz * dz)
        return functional(n, s), dx, dy, dz

    main = slice(fy, fy + inner)
    (e, e_n, e_s), dx, dy, dz = fields(fy, fy + inner, 0)
    e_ref[...] = e.reshape(fx, fy, fz)
    (_, _, s_low), dx_low, _, _ = fields(0, fy, 0)
    (_, _, s_high), dx_high, _, _ = fields(fy + inner, 2 * fy + inner, 0)
    (_, _, s_side), _, dy_side, _ = fields(2 * fy + inner, rows, 0)
    (_, _, s_end), _, _, dz_end = fields(fy, fy + inner, 1)
    flux_x = jnp.concatenate([s_low * dx_low, e_s * dx, s_high * dx_high], axis=0)
    change = flux_x[2 * fy :] - flux_x[: inner]
    flux_z, end_z = e_s * dz, s_end * dz_end
    lane = lax.broadcasted_iota(jnp.int32, (inner, fz), 1)
    after = pltpu.roll(jnp.where(lane == 0, end_z, flux_z), fz - 1, 1)
    before = pltpu.roll(jnp.where(lane == fz - 1, end_z, flux_z), 1, 1)
    change = change + (after - before)
    flux_y, side_y = e_s * dy, s_side * dy_side
    line = lax.broadcasted_iota(jnp.int32, (fy, fz), 0)
    for x in range(fx):
        here = slice(fy * x, fy * (x + 1))
        own = flux_y[here]
        after = jnp.where(line == fy - 1, side_y[fx + x : fx + x + 1], pltpu.roll(own, fy - 1, 0))
        before = jnp.where(line == 0, side_y[x : x + 1], pltpu.roll(own, 1, 0))
        v_ref[x] = e_n[here] - (2.0 * inv * inv) * (change[here] + (after - before))


def grid_terms(columns, left, right, nx, ny, nz):
    fx, fy, fz = 2 * nx, 2 * ny, 2 * nz
    vmem = pl.BlockSpec(memory_space=pltpu.VMEM)
    fine = jax.ShapeDtypeStruct((fx, fy, fz), jnp.float32)
    return pl.pallas_call(
        functools.partial(grid_kernel, fx, fy, fz),
        out_shape=(fine, fine),
        in_specs=[vmem] * 3,
        out_specs=(vmem, vmem),
        compiler_params=pltpu.CompilerParams(vmem_limit_bytes=32 << 20),
        cost_estimate=pl.CostEstimate(
            flops=300 * fx * fy * fz, transcendentals=10 * fx * fy * fz, bytes_accessed=2 << 20
        ),
        name="grid",
    )(columns, left, right)


def with_halo(cells, axis, dim, width, work, later=()):
    count = lax.axis_size(axis)
    even = lax.axis_index(axis) % 2 == 0
    head = lax.slice_in_dim(cells, 0, width, axis=dim)
    tail = lax.slice_in_dim(cells, cells.shape[dim] - width, cells.shape[dim], axis=dim)
    inner = [(i, i ^ 1) for i in range(count)]
    outer = [(i, (i + 1 if i % 2 else i - 1) % count) for i in range(count)]
    first = lax.ppermute(jnp.where(even, tail, head), axis, inner)
    second = lax.ppermute(jnp.where(even, head, tail), axis, outer)
    second, first, done, later = lax.optimization_barrier((second, first, work(), later))
    low, high = jnp.where(even, second, first), jnp.where(even, first, second)
    return jnp.concatenate([low, cells, high], axis=dim), done, later


def shards(
    coarse_density,
    atom_count,
    atom_species,
    density_matrix,
    partial_waves,
    smooth_waves,
    core_density,
    smooth_core,
):
    slots, pairs = density_matrix.shape[2:]
    nrad, npts = core_density.shape[1], partial_waves.shape[2]
    block = coarse_density.shape
    weights = tuple(jnp.asarray(w, jnp.bfloat16) for w in grid_tables(*block))
    cells, (lhs, line), partial_waves = with_halo(
        coarse_density, "gy", 1, 2,
        lambda: prepare(
            atom_species, density_matrix.reshape(slots, pairs), core_density, smooth_core, npts
        ),
        partial_waves,
    )
    cells, (*sums, left, right), smooth_waves = with_halo(
        cells, "gx", 0, 2,
        lambda: atom_terms(0, atom_count, atom_species, partial_waves, lhs, line, nrad, (), weights),
        smooth_waves,
    )
    cells, (placed, placed_energy), _ = with_halo(
        cells, "gz", 2, 2,
        lambda: atom_terms(1, atom_count, atom_species, smooth_waves, lhs, line, nrad, sums),
    )
    columns = cells.transpose(1, 0, 2).reshape(-1, cells.shape[2])
    potential, energy_density = grid_terms(columns, left, right, *block)
    return (
        potential,
        energy_density,
        placed.reshape(density_matrix.shape),
        placed_energy.reshape(atom_species.shape),
    )


def solution(mesh):
    in_specs = (
        P("gx", "gy", "gz"),
        P("gx", ("gy", "gz")),
        P("gx", ("gy", "gz"), None),
        P("gx", ("gy", "gz"), None, None),
        P(),
        P(),
        P(),
        P(),
    )
    out_specs = (
        P("gx", "gy", "gz"),
        P("gx", "gy", "gz"),
        P("gx", ("gy", "gz"), None, None),
        P("gx", ("gy", "gz"), None),
    )
    return jax.shard_map(shards, mesh=mesh, in_specs=in_specs, out_specs=out_specs, check_vma=False)
```

```python
import functools
import math

import jax
import jax.numpy as jnp
import numpy as np
from jax import lax
from jax.experimental import pallas as pl
from jax.experimental.pallas import tpu as pltpu
from jax.sharding import PartitionSpec as P

fine_step = 0.1
sphere_radius = 2.5
enhance_kappa = 0.804
enhance_mu = 0.2195149727645171
gradient_beta = 0.06672455060314922
gradient_gamma = (1.0 - math.log(2.0)) / math.pi**2
perdew_amplitude = 0.031091
perdew_alpha = 0.2137
perdew_first = 7.5957
perdew_second = 3.5876
perdew_third = 1.6382
perdew_fourth = 0.49294

exchange_scale = -0.75 * (3.0 / math.pi) ** (1.0 / 3.0)
fermi_scale = (3.0 * math.pi**2) ** (1.0 / 3.0)
radius_scale = (3.0 / (4.0 * math.pi)) ** (1.0 / 3.0)
reduced_scale = 1.0 / (4.0 * fermi_scale**2)
scaled_scale = math.pi / (16.0 * fermi_scale)
beta_ratio = gradient_beta / gradient_gamma
fit = [
    2.0 * perdew_amplitude * c * radius_scale ** (k / 2.0)
    for k, c in ((1, perdew_first), (2, perdew_second), (3, perdew_third), (4, perdew_fourth))
]
ln2 = math.log(2.0)
third = perdew_amplitude / 3.0


def functional(n, s):
    m = jnp.exp2(jnp.log2(n) * (-1.0 / 6.0))
    m2 = m * m
    m4 = m2 * m2
    m8 = m4 * m4
    by_p = (enhance_mu / enhance_kappa * reduced_scale) * (m8 * m8)
    by_t = (beta_ratio * scaled_scale) * (m8 * m4 * m2)
    fitted = m * (fit[0] + m * (fit[1] + m * (fit[2] + m * fit[3])))
    slope = m * (
        third * fit[0]
        + m * (2.0 * third * fit[1] + m * (3.0 * third * fit[2] + m * (4.0 * third * fit[3])))
    )
    one_fit = 1.0 + fitted
    enhance = 1.0 + s * by_p
    fit_both = fitted * one_fit
    joint = 1.0 / (fit_both * enhance)
    inverse_fit = joint * enhance
    damp = joint * fit_both
    log_term = jnp.log2(1.0 + one_fit * inverse_fit)
    alpha_r = (perdew_alpha * radius_scale) * m2
    one_alpha = 1.0 + alpha_r
    product_c = one_alpha * log_term
    inv_exp = 1.0 / (jnp.exp2((2.0 * perdew_amplitude / gradient_gamma) * product_c) - 1.0)
    c_n = (2.0 * ln2 * third) * (alpha_r * log_term) - one_alpha * (slope * inverse_fit)
    t = s * by_t
    q = t * inv_exp
    num = 1.0 + q
    den_inv = 1.0 / (1.0 + q * num)
    z = 1.0 + t * (num * den_inv)
    z_inv = 1.0 / z
    den_z = den_inv * z_inv
    h_t = ((num + q) * den_inv) * den_z
    h_c = (t * (q * den_inv)) * ((q * (1.0 + num)) * den_z) * (1.0 + inv_exp)
    ch = (gradient_gamma * ln2) * jnp.log2(z) - (2.0 * perdew_amplitude * ln2) * product_c
    x = (enhance_kappa * exchange_scale) * (n * m4)
    xf = x * ((1.0 + 1.0 / enhance_kappa) - damp)
    xd = x * damp
    e = n * (xf + ch)
    e_n = (
        (4.0 / 3.0) * xf
        + (8.0 / 3.0) * (xd * (damp - 1.0))
        + ch
        + (c_n - h_c * c_n)
        - (7.0 / 3.0 * gradient_gamma) * (h_t * t)
    )
    e_s = n * ((xd * damp) * by_p + gradient_gamma * (h_t * by_t))
    return e, e_n, e_s


ROW = 24


RADIAL = 8


def radial_table(nrad):
    g = np.arange(nrad)
    r = sphere_radius * (g + 0.5) / nrad
    k = nrad / sphere_radius
    up = np.where(g == nrad - 1, 0.0, np.where(g == 0, k, 0.5 * k))
    down = np.where(g == 0, 0.0, np.where(g == nrad - 1, -k, -0.5 * k))
    mid = np.where(g == 0, -k, np.where(g == nrad - 1, k, 0.0))
    rows = [r * r * (sphere_radius / nrad), up, mid, down, np.roll(up, 1), np.roll(down, -1)]
    return np.stack(rows + [np.zeros(nrad)] * 2).astype(np.float32)


def first_species(species_ref, na):
    row = lax.broadcasted_iota(jnp.int32, (na, 128), 0)
    species = jnp.zeros((na, 128), jnp.int32)
    for a in range(na):
        species = jnp.where(row == a, species_ref[0, 0, a], species)
    return species == 0


def prepare_kernel(
    ni, nrad, npts, na,
    species_ref, d_ref, ae_core_ref, ps_core_ref, radial_ref, lhs_ref, line_ref, lhs32,
):
    f32, bf16 = jnp.float32, jnp.bfloat16
    first_f = jnp.where(first_species(species_ref, na), 1.0, 0.0).astype(f32)
    second_f = 1.0 - first_f
    lhs32[...] = jnp.zeros_like(lhs32)
    for i in range(ni):
        d = d_ref[:, ni * i : ni * (i + 1)]
        d1 = d.astype(bf16).astype(f32)
        d2 = d - d1
        here = pl.ds(na * i, na)
        for block, part in ((0, d1), (1, d1), (2, d2)):
            at = 2 * ROW * block
            lhs32[here, at : at + ni] = part * first_f[:, :ni]
            lhs32[here, at + ROW : at + ROW + ni] = part * second_f[:, :ni]
    lhs_ref[...] = lhs32[:, 0 : 6 * ROW].astype(bf16)

    width = line_ref.shape[1]
    line_ref[0:2, 0:nrad] = ae_core_ref[...]
    line_ref[2:4, 0:nrad] = ps_core_ref[...]
    line_ref[4:RADIAL, 0:nrad] = jnp.ones((RADIAL - 4, nrad), f32)
    line_ref[RADIAL:, 0:nrad] = radial_ref[...]
    reach = nrad
    while reach < width:
        more = min(reach, width - reach)
        line_ref[:, reach : reach + more] = line_ref[:, 0:more]
        reach += more
    line_ref[RADIAL:, npts:] = jnp.zeros((8, width - npts), f32)


def prepare(species, matrices, ae_core, ps_core, npts):
    na, pairs = matrices.shape
    ni = math.isqrt(pairs)
    nrad = ae_core.shape[1]
    width = -(-npts // 128) * 128
    vmem = pl.BlockSpec(memory_space=pltpu.VMEM)
    smem = pl.BlockSpec(memory_space=pltpu.SMEM)
    f32, bf16 = jnp.float32, jnp.bfloat16
    return pl.pallas_call(
        functools.partial(prepare_kernel, ni, nrad, npts, na),
        out_shape=(
            jax.ShapeDtypeStruct((na * ni, 6 * ROW), bf16),
            jax.ShapeDtypeStruct((RADIAL + 8, width), f32),
        ),
        in_specs=[smem] + [vmem] * 4,
        out_specs=(vmem,) * 2,
        scratch_shapes=[pltpu.VMEM((na * ni, 256), f32)],
        compiler_params=pltpu.CompilerParams(vmem_limit_bytes=8 << 20),
        cost_estimate=pl.CostEstimate(flops=1 << 31, transcendentals=0, bytes_accessed=6 << 20),
        name="prepare",
    )(species, matrices, ae_core, ps_core, jnp.asarray(radial_table(nrad)))


def atoms_kernel(
    ni, nrad, npts, na, table, runs, has_sums, carried,
    count_ref, species_ref, x_ref, lhs_ref, line_ref, *refs,
):
    f32, bf16 = jnp.float32, jnp.bfloat16
    if has_sums:
        h_in_ref, e_in_ref, *refs = refs
    carry_in, (h_ref, e_ref, *refs) = refs[:carried], refs[carried:]
    carry_out, (total, *scratch) = refs[:carried], refs[carried:]
    for source, target in zip(carry_in, carry_out):
        target[...] = source[...]
    first = first_species(species_ref, na)
    row = lax.broadcasted_iota(jnp.int32, (na, 128), 0)

    e_sum = jnp.zeros((na, 128), f32)
    for u, (low, high) in enumerate(runs):
        waves, packed, rho, part_q = scratch[4 * u : 4 * u + 4]
        size, live = high - low, min(high, npts) - low
        tail = live // 128 * 128
        if tail < size:
            waves[:, tail:] = jnp.zeros((2 * ROW, size - tail), f32)
        for s in range(2):
            waves[ROW * s + 16 : ROW * (s + 1), 0:tail] = jnp.zeros((ROW - 16, tail), f32)
            waves[ROW * s : ROW * s + ni, 0:live] = x_ref[s, :, low : low + live]
        pick = jnp.concatenate([first] * (size // 128), axis=1)

        x = waves[...]
        x1 = x.astype(bf16)
        x2 = (x - x1.astype(f32)).astype(bf16)
        packed[...] = jnp.concatenate([x1, x2], axis=0)
        mixed = jnp.dot(
            lhs_ref[...], jnp.concatenate([x1, x2, x1], axis=0), preferred_element_type=f32
        )
        n = jnp.where(
            pick,
            line_ref[2 * table : 2 * table + 1, low:high],
            line_ref[2 * table + 1 : 2 * table + 2, low:high],
        )
        for i in range(ni):
            own = jnp.where(pick, x[i : i + 1], x[ROW + i : ROW + i + 1])
            n = n + own * mixed[na * i : na * (i + 1)]
        rho[...] = n

        scale = (-1.0 if table else 1.0) * 4.0 * math.pi * nrad / npts
        n = rho[...]
        radial = line_ref[RADIAL:, low:high]
        weight = radial[0:1] * scale
        up, mid, down = radial[1:2], radial[2:3], radial[3:4]
        slope = up * pltpu.roll(n, size - 1, 1) + mid * n + down * pltpu.roll(n, 1, 1)
        e, e_n, e_s = functional(n, slope * slope)
        we = e * weight
        for j in range(size // 128):
            e_sum = e_sum + we[:, 128 * j : 128 * (j + 1)]
        part_q[...] = (slope * e_s) * (2.0 * weight)
        q = part_q[...]
        g = e_n * weight + mid * q
        g = g + radial[4:5] * pltpu.roll(q, 1, 1) + radial[5:6] * pltpu.roll(q, size - 1, 1)
        rho[...] = g
        g = rho[...]
        x = waves[...]
        hi, lo = [], []
        for i in range(ni):
            own = jnp.where(pick, x[i : i + 1], x[ROW + i : ROW + i + 1]) * g
            top = own.astype(bf16)
            hi.append(top)
            lo.append((own - top.astype(f32)).astype(bf16))
        out = lax.dot_general(
            jnp.concatenate(hi + lo, axis=0), packed[...], (((1,), (1,)), ((), ())),
            preferred_element_type=f32,
        )
        if u == 0:
            total[...] = out
        else:
            total[...] += out

    tally = count_ref[0, 0]
    live = row < tally
    for i in range(ni):
        both = total[na * i : na * (i + 1), :] + total[na * (ni + i) : na * (ni + i + 1), :]
        value = both[:, 0 : 2 * ROW] + both[:, 2 * ROW : 4 * ROW]
        value = jnp.where(first[:, :ni], value[:, 0:ni], value[:, ROW : ROW + ni])
        here = slice(ni * i, ni * (i + 1))
        value = jnp.where(live[:, :ni], value, 0.0)
        h_ref[:, here] = h_in_ref[:, here] + value if has_sums else value
    energy = jnp.sum(e_sum, axis=1, keepdims=True)
    energy = jnp.where(live[:, :1], energy, 0.0)
    diagonal = lax.broadcasted_iota(jnp.int32, (na, na), 0) == lax.broadcasted_iota(
        jnp.int32, (na, na), 1
    )
    energy = jnp.sum(jnp.where(diagonal, energy, 0.0), axis=0, keepdims=True)
    e_ref[...] = e_in_ref[...] + energy if has_sums else energy


def atom_terms(table, count, species, x, lhs, line, nrad, sums=(), carry=()):
    _, ni, npts = x.shape
    na = lhs.shape[0] // ni
    width = line.shape[1]
    runs = [(0, width)]
    vmem = pl.BlockSpec(memory_space=pltpu.VMEM)
    smem = pl.BlockSpec(memory_space=pltpu.SMEM)
    f32, bf16 = jnp.float32, jnp.bfloat16
    scratch = [pltpu.VMEM((2 * na * ni, 4 * ROW), f32)]
    for low, high in runs:
        scratch += [
            pltpu.VMEM((2 * ROW, high - low), f32),
            pltpu.VMEM((4 * ROW, high - low), bf16),
            pltpu.VMEM((na, high - low), f32),
            pltpu.VMEM((na, high - low), f32),
        ]
    return pl.pallas_call(
        functools.partial(atoms_kernel, ni, nrad, npts, na, table, runs, bool(sums), len(carry)),
        out_shape=(
            jax.ShapeDtypeStruct((na, ni * ni), f32),
            jax.ShapeDtypeStruct((1, na), f32),
            *(jax.ShapeDtypeStruct(c.shape, c.dtype) for c in carry),
        ),
        in_specs=[smem, smem] + [vmem] * (3 + len(sums) + len(carry)),
        out_specs=(vmem,) * (2 + len(carry)),
        scratch_shapes=scratch,
        compiler_params=pltpu.CompilerParams(vmem_limit_bytes=32 << 20),
        cost_estimate=pl.CostEstimate(
            flops=4 * na * ni * ni * npts, transcendentals=na * npts * 10, bytes_accessed=2 << 20
        ),
        name="atoms",
    )(count, species, x, lhs, line, *sums, *carry)


def upsampling(cells, halo):
    table = np.zeros((2 * cells + 4, cells + 2 * halo))
    for k in range(-2, 2 * cells + 2):
        i = k // 2
        table[k + 2, i + halo] = 0.75
        table[k + 2, i + halo + (1 if k % 2 else -1)] = 0.25
    return table


def grid_tables(nx, ny, nz):
    ux, uy, uz = upsampling(nx, 2), upsampling(ny, 2), upsampling(nz, 2)
    fx, fy, fz = 2 * nx, 2 * ny, 2 * nz

    def diff(u):
        return np.concatenate([np.zeros_like(u[:1]), u[2:] - u[:-2], np.zeros_like(u[:1])])

    places = [(-1, y) for y in range(fy)]
    places += [(x, y) for x in range(fx) for y in range(fy)]
    places += [(fx, y) for y in range(fy)]
    places += [(x, -1) for x in range(fx)] + [(x, fy) for x in range(fx)]

    def rows(wx, wy):
        return np.stack([np.outer(wy[y + 2], wx[x + 2]).reshape(-1) for x, y in places])

    left = np.concatenate([rows(ux, uy), rows(diff(ux), uy), rows(ux, diff(uy))])
    beyond = np.array([fz] + [fz // 2] * (fz - 2) + [-1])
    right = np.concatenate(
        [w[at + 2] for w in (uz, diff(uz)) for at in (np.arange(fz), beyond)]
    ).T
    return np.concatenate([left] * 3, axis=1), right


def split3(x):
    f32, bf16 = jnp.float32, jnp.bfloat16
    x1 = x.astype(bf16)
    rest = x - x1.astype(f32)
    x2 = rest.astype(bf16)
    return x1, x2, (rest - x2.astype(f32)).astype(bf16)


def grid_kernel(fx, fy, fz, c_ref, left_ref, right_ref, v_ref, e_ref):
    f32 = jnp.float32
    right = right_ref[...]
    parts = [jnp.dot(p, right, preferred_element_type=f32) for p in split3(c_ref[...])]
    lines = parts[0] + (parts[1] + parts[2])
    stack = jnp.concatenate(split3(lines), axis=0)
    inner = fx * fy
    rows = inner + 2 * fy + 2 * fx
    plane = jnp.dot(left_ref[...], stack[:, : 2 * fz], preferred_element_type=f32)
    dz_all = jnp.dot(left_ref[0:rows, :], stack[:, 2 * fz :], preferred_element_type=f32)
    inv = 0.5 / fine_step

    def fields(lo, hi, tile):
        cols = slice(fz * tile, fz * (tile + 1))
        n, dx, dy = (plane[rows * k + lo : rows * k + hi, cols] for k in range(3))
        dz = dz_all[lo:hi, cols]
        s = (inv * inv) * (dx * dx + dy * dy + dz * dz)
        return functional(n, s), dx, dy, dz

    main = slice(fy, fy + inner)
    (e, e_n, e_s), dx, dy, dz = fields(fy, fy + inner, 0)
    e_ref[...] = e.reshape(fx, fy, fz)
    (_, _, s_low), dx_low, _, _ = fields(0, fy, 0)
    (_, _, s_high), dx_high, _, _ = fields(fy + inner, 2 * fy + inner, 0)
    (_, _, s_side), _, dy_side, _ = fields(2 * fy + inner, rows, 0)
    (_, _, s_end), _, _, dz_end = fields(fy, fy + inner, 1)
    flux_x = jnp.concatenate([s_low * dx_low, e_s * dx, s_high * dx_high], axis=0)
    change = flux_x[2 * fy :] - flux_x[: inner]
    flux_z, end_z = e_s * dz, s_end * dz_end
    lane = lax.broadcasted_iota(jnp.int32, (inner, fz), 1)
    after = pltpu.roll(jnp.where(lane == 0, end_z, flux_z), fz - 1, 1)
    before = pltpu.roll(jnp.where(lane == fz - 1, end_z, flux_z), 1, 1)
    change = change + (after - before)
    flux_y, side_y = e_s * dy, s_side * dy_side
    line = lax.broadcasted_iota(jnp.int32, (fy, fz), 0)
    for x in range(fx):
        here = slice(fy * x, fy * (x + 1))
        own = flux_y[here]
        after = jnp.where(line == fy - 1, side_y[fx + x : fx + x + 1], pltpu.roll(own, fy - 1, 0))
        before = jnp.where(line == 0, side_y[x : x + 1], pltpu.roll(own, 1, 0))
        v_ref[x] = e_n[here] - (2.0 * inv * inv) * (change[here] + (after - before))


def grid_terms(columns, left, right, nx, ny, nz):
    fx, fy, fz = 2 * nx, 2 * ny, 2 * nz
    vmem = pl.BlockSpec(memory_space=pltpu.VMEM)
    fine = jax.ShapeDtypeStruct((fx, fy, fz), jnp.float32)
    return pl.pallas_call(
        functools.partial(grid_kernel, fx, fy, fz),
        out_shape=(fine, fine),
        in_specs=[vmem] * 3,
        out_specs=(vmem, vmem),
        compiler_params=pltpu.CompilerParams(vmem_limit_bytes=32 << 20),
        cost_estimate=pl.CostEstimate(
            flops=300 * fx * fy * fz, transcendentals=10 * fx * fy * fz, bytes_accessed=2 << 20
        ),
        name="grid",
    )(columns, left, right)


def with_halo(cells, axis, dim, width, work, later=()):
    count = lax.axis_size(axis)
    even = lax.axis_index(axis) % 2 == 0
    head = lax.slice_in_dim(cells, 0, width, axis=dim)
    tail = lax.slice_in_dim(cells, cells.shape[dim] - width, cells.shape[dim], axis=dim)
    inner = [(i, i ^ 1) for i in range(count)]
    outer = [(i, (i + 1 if i % 2 else i - 1) % count) for i in range(count)]
    first = lax.ppermute(jnp.where(even, tail, head), axis, inner)
    second = lax.ppermute(jnp.where(even, head, tail), axis, outer)
    second, first, done, later = lax.optimization_barrier((second, first, work(), later))
    low, high = jnp.where(even, second, first), jnp.where(even, first, second)
    return jnp.concatenate([low, cells, high], axis=dim), done, later


def shards(
    coarse_density,
    atom_count,
    atom_species,
    density_matrix,
    partial_waves,
    smooth_waves,
    core_density,
    smooth_core,
):
    slots, pairs = density_matrix.shape[2:]
    nrad, npts = core_density.shape[1], partial_waves.shape[2]
    block = coarse_density.shape
    weights = tuple(jnp.asarray(w, jnp.bfloat16) for w in grid_tables(*block))
    cells, (lhs, line), partial_waves = with_halo(
        coarse_density, "gy", 1, 2,
        lambda: prepare(
            atom_species, density_matrix.reshape(slots, pairs), core_density, smooth_core, npts
        ),
        partial_waves,
    )
    cells, (*sums, left, right), smooth_waves = with_halo(
        cells, "gx", 0, 2,
        lambda: atom_terms(0, atom_count, atom_species, partial_waves, lhs, line, nrad, (), weights),
        smooth_waves,
    )
    cells, (placed, placed_energy), _ = with_halo(
        cells, "gz", 2, 2,
        lambda: atom_terms(1, atom_count, atom_species, smooth_waves, lhs, line, nrad, sums),
    )
    columns = cells.transpose(1, 0, 2).reshape(-1, cells.shape[2])
    potential, energy_density = grid_terms(columns, left, right, *block)
    return (
        potential,
        energy_density,
        placed.reshape(density_matrix.shape),
        placed_energy.reshape(atom_species.shape),
    )


def solution(mesh):
    in_specs = (
        P("gx", "gy", "gz"),
        P("gx", ("gy", "gz")),
        P("gx", ("gy", "gz"), None),
        P("gx", ("gy", "gz"), None, None),
        P(),
        P(),
        P(),
        P(),
    )
    out_specs = (
        P("gx", "gy", "gz"),
        P("gx", "gy", "gz"),
        P("gx", ("gy", "gz"), None, None),
        P("gx", ("gy", "gz"), None),
    )
    return jax.shard_map(shards, mesh=mesh, in_specs=in_specs, out_specs=out_specs, check_vma=False)
```
